32 devices in a mesh: tile: 8 (over z, x), aux: 4 (over y, core).
Axes of the slice: x: 2, y: 2, z: 4, core: 2. Of those that a mesh axis runs over, the one named last changes fastest.
Arguments:
- density: float32 [1024, 1024], P('tile', 'aux'), may hold values from -6 to 6
- factors: float32 [192, 16, 128, 128], P(('tile', 'aux')), may hold values from -0.125 to 0.125
- orthogonalizers: float32 [1024, 128], replicated, may hold values from -0.5 to 0.5
- slot_pairs: int32 [1024, 2], P(('tile', 'aux')), may hold values from 0 to 5
- density_source: int32 [1024, 1], replicated, may hold values from 0 to 7; in each aligned block of 32 rows (0 to 31, 32 to 63, ...) at most 8 rows name the same one
- density_column: int32 [1024, 1], replicated, may hold values from 0 to 7
- target_row: int32 [1024, 1], replicated, may hold values from 0 to 7; in each aligned block of 32 rows (0 to 31, 32 to 63, ...) at most 8 rows name the same one
- target_column: int32 [1024, 1], replicated, may hold values from 0 to 7
Outputs:
- fock_exchange: float32 [1024, 1024], P('tile', 'aux')
The draws below stay inside these ranges and needn't reach their ends.
Inputs may be any that keep to these rules, and one draw needn't show every extreme that they name: `density_source`: in each aligned block of 32 rows (the tasks of one device) no row tile is named more than 8 times, a bound that some block reaches. `target_row`: in each aligned block of 32 rows (the tasks of one device) no row tile is named more than 8 times, a bound that some block reaches.
All inputs are finite; a program needn't handle non-finite values.
Results may differ from the reference program's by a relative error of at most 0.0001.
Values sent between devices are 32-bit elements; how exact they have to be, the bound alone decides.
No kernel may reach another device: no remote copies, remote signals or barrier semaphores. Data moves between devices by JAX's collectives and lax.ppermute only.
A program may use at most 128 MiB of HBM per device.

```python
import math
import jax
import jax.numpy as jnp
import numpy as np
from jax import lax

TILE = 128
AUX_DEV = 16
SLOTS = 6
TASKS_DEV = 32
CAP = 8
NBF = 1024
ROWS = 1024
N_TILE = 8


def place_ends(values, stream_key, low, top_value):
    spot = [jax.random.randint(jax.random.fold_in(stream_key, axis), (), 0, length) for axis, length in enumerate(values.shape)]
    longest = values.shape.index(max(values.shape))
    neighbour = spot[:longest] + [(spot[longest] + 1) % values.shape[longest]] + spot[longest + 1:]
    return values.at[tuple(spot)].set(low).at[tuple(neighbour)].set(top_value)


def block_scale(key, dims, split, smallest, high):
    level = 1.0
    for axis_at, parts in split:
        steps = jax.random.uniform(jax.random.fold_in(jax.random.fold_in(key, 6), axis_at), (parts,), jnp.float32, smallest / len(split), high / len(split))
        level = level * jnp.repeat(jnp.exp(steps), dims[axis_at] // parts).reshape((-1,) + (1,) * (len(dims) - 1 - axis_at))
    return level


def routed_block(rng, own, number, rows, amount, top, bound, slope):
    sequence = jax.random.permutation(rng, amount)
    packed, usual = shares(amount, rows * top, bound, slope, True), shares(amount, rows * top, bound, slope, False)
    places = jnp.arange(amount)

    def named(lengths, turn):
        used = int((lengths > 0).sum())
        fixed = max(1, used // 4)
        shifted = fixed + (places - fixed + turn * (used - fixed)) % max(1, amount - fixed)
        return jnp.zeros((amount,), jnp.int32).at[sequence[jnp.where(places < fixed, places, shifted)]].set(jnp.asarray(lengths, jnp.int32))

    lengths = jnp.where(number % 4 == 0, named(packed, number // 4), named(usual, number - number // 4 - 1))
    mixed = jax.random.permutation(jax.random.fold_in(own, 3), amount)
    source_of, taker = mixed[0:amount // 2 * 2:2], mixed[1:amount // 2 * 2:2]
    margin = jnp.minimum(lengths[source_of] - 1, bound - lengths[taker]) // 2
    margin = jnp.where((source_of == sequence[0]) | (taker == sequence[0]) | (lengths[taker] == 0), 0, jnp.maximum(margin, 0))
    shifted = jax.random.randint(jax.random.fold_in(own, 4), (amount // 2,), 0, 1 << 20) % (margin + 1)
    lengths = lengths.at[source_of].add(-shifted).at[taker].add(shifted)
    labels = jnp.searchsorted(jnp.cumsum(lengths), jnp.arange(rows * top), side="right").astype(jnp.int32)
    grid = labels.reshape(top, rows).T
    grid = grid[jax.random.permutation(jax.random.fold_in(own, 1), rows)]
    turn = jax.random.randint(jax.random.fold_in(own, 2), (rows, 1), 0, top)
    return jnp.take_along_axis(grid, (jnp.arange(top)[None, :] + turn) % top, axis=1)


def shares(count, total, limit, skew, full):
    weights = [(1 << 20) // math.isqrt(standing ** skew) + 1 for standing in range(1, count + 1)]
    largest = limit if full else min(limit, max(-(-total // count), total * weights[0] // sum(weights)))
    least = 1 if total - largest >= count - 1 else 0
    holding, spare = [largest] + [least] * (count - 1), total - largest - least * (count - 1)
    while spare > 0:
        candidates = [i for i in range(1, count) if holding[i] < largest] or [i for i in range(1, count) if holding[i] < limit]
        pool, left = sum([weights[i] for i in candidates]), spare
        for i in candidates:
            extra = min(limit - holding[i], max(1, left * weights[i] // pool), spare)
            holding[i] = holding[i] + extra
            spare = spare - extra
    return np.array(holding)


def bell_draw(rng, dims, scale, bound, split=(), held_as=jnp.bfloat16):
    drawn = scale * jax.random.normal(rng, dims, jnp.float32)
    if split:
        drawn = drawn * block_scale(rng, dims, split, -0.22, 0.18)
    return jnp.clip(drawn, -bound, bound).astype(held_as)


def setup_inputs(seed: int = 0) -> dict:
    splits = jax.random.split(jax.random.key(seed), 9)
    density = bell_draw(splits[0], (NBF, NBF), 1.0, 6.0, ((0, 8), (1, 4)), jnp.float32)
    factors = bell_draw(splits[1], (ROWS // TASKS_DEV * SLOTS, AUX_DEV, TILE, TILE), (TILE * AUX_DEV) ** -0.5, 0.125, ((0, 32),), jnp.float32)
    orthogonalizers = bell_draw(splits[2], (NBF, TILE), TILE ** -0.5, 0.5, (), jnp.float32)
    slot_pairs = place_ends(jax.random.randint(splits[3], (ROWS, 2), 0, SLOTS), jax.random.fold_in(splits[3], 1), 0, SLOTS - 1).astype(jnp.int32)
    density_source_keys = jax.random.split(jax.random.fold_in(splits[4], 1), ROWS // TASKS_DEV)
    density_source_turns = jax.random.permutation(jax.random.fold_in(splits[4], 3), ROWS // TASKS_DEV)
    density_source = jax.vmap(lambda own, number: routed_block(jax.random.fold_in(splits[4], 2), own, number, TASKS_DEV, N_TILE, 1, CAP, 2))(density_source_keys, density_source_turns).reshape((ROWS, 1))
    density_column = place_ends(jax.random.randint(splits[5], (ROWS, 1), 0, N_TILE), jax.random.fold_in(splits[5], 1), 0, N_TILE - 1).astype(jnp.int32)
    target_row_keys = jax.random.split(jax.random.fold_in(splits[6], 1), ROWS // TASKS_DEV)
    target_row_turns = jax.random.permutation(jax.random.fold_in(splits[6], 3), ROWS // TASKS_DEV)
    target_row = jax.vmap(lambda own, number: routed_block(jax.random.fold_in(splits[6], 2), own, number, TASKS_DEV, N_TILE, 1, CAP, 2))(target_row_keys, target_row_turns).reshape((ROWS, 1))
    target_column = place_ends(jax.random.randint(splits[7], (ROWS, 1), 0, N_TILE), jax.random.fold_in(splits[7], 1), 0, N_TILE - 1).astype(jnp.int32)
    return {"density": density, "factors": factors, "orthogonalizers": orthogonalizers, "slot_pairs": slot_pairs, "density_source": density_source, "density_column": density_column, "target_row": target_row, "target_column": target_column}


def reference(density, factors, orthogonalizers, slot_pairs, density_source, density_column, target_row, target_column):
    highest = lax.Precision.HIGHEST
    density_tiles = density.reshape(N_TILE, TILE, N_TILE, TILE)
    rows_all = slot_pairs.shape[0]
    device_of = jnp.arange(rows_all, dtype=jnp.int32) // TASKS_DEV
    left_index = (device_of * SLOTS + slot_pairs[:, 0]).astype(jnp.int32)
    right_index = (device_of * SLOTS + slot_pairs[:, 1]).astype(jnp.int32)
    columns = (left_index, right_index, density_source[:, 0], density_column[:, 0], target_row[:, 0], target_column[:, 0])
    blocks = tuple(value.astype(jnp.int32).reshape(-1, TASKS_DEV) for value in columns)

    def step(exchange_sum, block):
        lefts, rights, rows_c, cols_d, rows_a, cols_b = block
        dens_block = density_tiles[rows_c, :, cols_d, :]
        halfway = jnp.einsum("gpik,gkl->gpil", factors[lefts], dens_block, precision=highest)
        partial_value = jnp.einsum("gpil,gplj->gij", halfway, factors[rights], precision=highest)
        return exchange_sum.at[rows_a, cols_b].add(partial_value), None

    exchange_sum = jnp.zeros((N_TILE, N_TILE, TILE, TILE), jnp.float32)
    exchange_sum, unused = lax.scan(step, exchange_sum, blocks)
    symmetric = exchange_sum + jnp.transpose(exchange_sum, (1, 0, 3, 2))
    blocks_x = orthogonalizers.reshape(N_TILE, TILE, TILE)
    leftward = jnp.einsum("aki,abkl->abil", blocks_x, symmetric, precision=highest)
    fock = jnp.einsum("abil,blj->abij", leftward, blocks_x, precision=highest)
    return jnp.transpose(fock, (0, 2, 1, 3)).reshape(N_TILE * TILE, N_TILE * TILE)
```

```python
import functools

import jax
import jax.numpy as jnp
from jax import lax
from jax.experimental import pallas as pl
from jax.experimental.pallas import tpu as pltpu
from jax.sharding import PartitionSpec as P

highest = lax.Precision.HIGHEST
AXES = ("tile", "aux")
GATHER_LIMIT = 16 << 20


def ranks_of(key_rows):
    task_count = key_rows.shape[-1]
    position = jnp.arange(task_count)
    earlier = position[None, :] < position[:, None]
    matching = key_rows[..., :, None] == key_rows[..., None, :]
    return jnp.sum(matching & earlier, axis=-1)


def slot_table(key_rows, other_rows, wanted, capacity):
    ranking = ranks_of(key_rows)
    levels = jnp.arange(capacity)
    chosen = (key_rows == wanted)[..., None, :] & (ranking[..., None, :] == levels[:, None])
    picked = jnp.sum(jnp.where(chosen, other_rows[..., None, :], 0), axis=-1)
    filled = jnp.any(chosen, axis=-1)
    return (picked, filled)


def routed(
    density,
    factors,
    orthogonalizers,
    slot_pairs,
    density_source,
    density_column,
    target_row,
    target_column,
):
    tiles_all = lax.axis_size("tile")
    aux_count = lax.axis_size("aux")
    tile_me = lax.axis_index("tile")
    aux_me = lax.axis_index("aux")
    tile_width = factors.shape[-1]
    task_count = slot_pairs.shape[0]
    capacity = max(2, 2 * task_count // tiles_all)
    quarter = tile_width // aux_count
    per_block = tiles_all // aux_count
    source_grid = density_source.reshape(tiles_all, aux_count, task_count)
    column_grid = density_column.reshape(tiles_all, aux_count, task_count)
    target_grid = target_row.reshape(tiles_all, aux_count, task_count)
    target_cols = target_column.reshape(tiles_all, aux_count, task_count)
    own_source = source_grid[tile_me, aux_me]
    own_target = target_grid[tile_me, aux_me]
    row_slab = lax.all_gather(density, "aux", axis=1, tiled=True)
    slab_tiles = row_slab.reshape(tile_width, tiles_all, tile_width)
    group_source = lax.dynamic_index_in_dim(source_grid, aux_me, 1, False)
    group_column = lax.dynamic_index_in_dim(column_grid, aux_me, 1, False)
    send_cols, send_filled = slot_table(group_source, group_column, tile_me, capacity)
    outgoing = jnp.take(slab_tiles, send_cols, axis=1)
    outgoing = jnp.where(send_filled[None, :, :, None], outgoing, 0.0)
    incoming = lax.all_to_all(outgoing, "tile", split_axis=1, concat_axis=1, tiled=True)
    own_rank = ranks_of(own_source)
    group = 8
    batches = task_count // group

    def one_batch(items):
        sources, rank_block, lefts, rights = items
        dens_block = incoming[:, sources, rank_block, :]
        halfway = jnp.einsum("gpik,kgl->gpil", factors[lefts], dens_block, precision=highest)
        return jnp.einsum("gpil,gplj->gij", halfway, factors[rights], precision=highest)

    partials = lax.map(
        one_batch,
        (
            own_source.reshape(batches, group),
            own_rank.reshape(batches, group),
            slot_pairs[:, 0].reshape(batches, group),
            slot_pairs[:, 1].reshape(batches, group),
        ),
    )
    partials = partials.reshape(task_count, tile_width, tile_width)
    task_ids = jnp.arange(task_count, dtype=jnp.int32)
    owners = jnp.arange(tiles_all, dtype=jnp.int32)[:, None]
    send_task, send_live = slot_table(own_target[None, :], task_ids[None, :], owners, capacity)
    outbound = jnp.where(send_live[:, :, None, None], partials[send_task], 0.0)
    arrived = lax.all_to_all(outbound, "tile", split_axis=0, concat_axis=0, tiled=True)
    group_target = lax.dynamic_index_in_dim(target_grid, aux_me, 1, False)
    group_cols = lax.dynamic_index_in_dim(target_cols, aux_me, 1, False)
    cols_b, cols_live = slot_table(group_target, group_cols, tile_me, capacity)
    spread = ((cols_b.reshape(-1)[None, :] == owners) & cols_live.reshape(-1)[None, :]).astype(
        jnp.float32
    )
    row_sums = jnp.einsum(
        "bs,sij->ibj", spread, arrived.reshape(-1, tile_width, tile_width), precision=highest
    )
    row_sums = row_sums.reshape(tile_width, tiles_all * tile_width)
    exchange_rows = lax.psum_scatter(row_sums, "aux", scatter_dimension=0, tiled=True)
    mirrored = lax.all_to_all(
        lax.all_to_all(
            exchange_rows.reshape(quarter, tiles_all, tile_width),
            "tile",
            split_axis=1,
            concat_axis=1,
            tiled=True,
        ),
        "aux",
        split_axis=1,
        concat_axis=0,
        tiled=True,
    )
    full_rows = lax.all_to_all(
        exchange_rows.reshape(quarter, aux_count, per_block * tile_width),
        "aux",
        split_axis=1,
        concat_axis=0,
        tiled=True,
    )
    direct_part = full_rows.reshape(tile_width, per_block, tile_width)
    symmetric = direct_part + jnp.transpose(mirrored, (2, 1, 0))
    blocks_x = orthogonalizers.reshape(tiles_all, tile_width, tile_width)
    left_x = blocks_x[tile_me]
    right_x = lax.dynamic_slice_in_dim(blocks_x, aux_me * per_block, per_block, 0)
    leftward = jnp.einsum("ki,kbl->ibl", left_x, symmetric, precision=highest)
    fock = jnp.einsum("ibl,blj->ibj", leftward, right_x, precision=highest)
    return fock.reshape(tile_width, per_block * tile_width)


def split(x):
    hi = x.astype(jnp.bfloat16)
    lo = (x - hi.astype(jnp.float32)).astype(jnp.bfloat16)
    return hi, lo

def prep_kernel(f_ref, o_ref):
    hi, lo = split(f_ref[0])
    w = hi.shape[-1]
    o_ref[0, :, :w] = hi
    o_ref[0, :, w:] = lo

def prep(factors, block=1024):
    s, p, w, _ = factors.shape
    rows = p * w
    return pl.pallas_call(
        prep_kernel,
        grid=(s, rows // block),
        in_specs=[pl.BlockSpec((1, block, w), lambda i, j: (i, j, 0))],
        out_specs=pl.BlockSpec((1, block, 2 * w), lambda i, j: (i, j, 0)),
        out_shape=jax.ShapeDtypeStruct((s, rows, 2 * w), jnp.bfloat16),
        cost_estimate=pl.CostEstimate(flops=2 * factors.size, bytes_accessed=8 * factors.size, transcendentals=0),
    )(factors.reshape(s, rows, w))

def task_kernel(w, tab, f2_hbm, *refs):
    ng = (len(refs) - 7)
    gs = refs[:-5]; out, f2, dv, fsem, gsem = refs[-5:]
    tasks = tab.shape[1]
    shards = gs[0].shape[0]
    slots = f2.shape[0]
    for s in range(slots):
        pltpu.make_async_copy(f2_hbm.at[s], f2.at[s], fsem.at[s]).start()
    for i, g in enumerate(gs):
        pltpu.make_async_copy(g, dv.at[pl.ds(i * shards, shards)], gsem.at[i]).start()
    out[...] = jnp.zeros_like(out)
    for i, g in enumerate(gs):
        pltpu.make_async_copy(g, dv.at[pl.ds(i * shards, shards)], gsem.at[i]).wait()
    for s in range(slots):
        pltpu.make_async_copy(f2_hbm.at[s], f2.at[s], fsem.at[s]).wait()
    pairs = f2.shape[1] // (2 * w)

    def task(q, carry):
        left, right = tab[0, q], tab[1, q]
        dsh, dcol = tab[2, q], pl.multiple_of(tab[3, q] * w, w)
        hi, lo = split(dv[dsh, :, pl.ds(dcol, w)])
        half = jnp.concatenate([hi, lo], axis=1)
        wt = jnp.concatenate([half, half], axis=0)
        acc = jnp.zeros((2 * w, 2 * w), jnp.float32)
        for p in range(pairs):
            rows = slice(p * 2 * w, (p + 1) * 2 * w)
            h = jnp.dot(f2[left, rows, :], wt, preferred_element_type=jnp.float32)
            hi, lo = split(h[:, :w] + h[:, w:])
            lhs = jnp.concatenate([jnp.concatenate([hi[:w], hi[w:]], axis=1), jnp.concatenate([lo[:w], lo[w:]], axis=1)], axis=0)
            acc = acc + jnp.dot(lhs, f2[right, rows, :], preferred_element_type=jnp.float32)
        part = acc[:w] + acc[w:]
        part = part[:, :w] + part[:, w:]
        c1 = pl.ds(pl.multiple_of(tab[5, q] * w, w), w)
        out[tab[4, q], :, c1] = out[tab[4, q], :, c1] + part
        c2 = pl.ds(pl.multiple_of(tab[7, q] * w, w), w)
        out[tab[6, q], :, c2] = out[tab[6, q], :, c2] + part.T
        return carry

    lax.fori_loop(0, tasks, task, 0)

def run_tasks(tab, f2, gathered):
    w = gathered[0].shape[1]
    n = sum(g.shape[0] for g in gathered)
    tasks = tab.shape[1]
    slots, rows, _ = f2.shape
    shape = (n,) + gathered[0].shape[1:]
    return pl.pallas_call(
        functools.partial(task_kernel, w),
        grid_spec=pltpu.PrefetchScalarGridSpec(
            num_scalar_prefetch=1, grid=(1,),
            in_specs=[pl.BlockSpec(memory_space=pl.ANY)] * (1 + len(gathered)),
            out_specs=pl.BlockSpec(shape, lambda i, t: (0, 0, 0), pipeline_mode=pl.Buffered(1)),
            scratch_shapes=[pltpu.VMEM(f2.shape, f2.dtype), pltpu.VMEM(shape, jnp.float32),
                pltpu.SemaphoreType.DMA((slots,)), pltpu.SemaphoreType.DMA((len(gathered),))]),
        out_shape=jax.ShapeDtypeStruct(shape, jnp.float32),
        cost_estimate=pl.CostEstimate(flops=tasks * rows * w * w * 16, bytes_accessed=2 * f2.size + 8 * n * w * 2 * w, transcendentals=0),
    )(tab, f2, *gathered)


def grid_of(tiles_all, aux_count):
    return tiles_all // 2, 2, aux_count // 2, 2


def shift(value, sizes, move):
    depth, wide, tall, cores = sizes
    pairs = []
    for source in range(depth * wide * tall * cores):
        rest, c = divmod(source, cores)
        rest, y = divmod(rest, tall)
        z, x = divmod(rest, wide)
        tz, tx, ty, tc = move(z, x, y, c)
        pairs.append((source, (((tz % depth) * wide + tx) * tall + ty) * cores + tc))
    return lax.ppermute(value, AXES, pairs)


def across_x(z, x, y, c):
    return z, 1 - x, y, c


def across_y(z, x, y, c):
    return z, x, 1 - y, c


def across_core(z, x, y, c):
    return z, x, y, 1 - c


def across_diagonal(z, x, y, c):
    return (z, x, 1 - y, c) if c == 0 else (z, 1 - x, y, c)


def gather_shards(own, sizes, core_me):
    depth = sizes[0]
    column = [own]
    for step in range(1, depth):
        column.append(shift(own, sizes, lambda z, x, y, c, step=step: (z + step, x, y, c)))
    here = jnp.stack(column)
    side_x = shift(here, sizes, across_x)
    side_y = shift(here, sizes, across_y)
    corner = shift(jnp.where(core_me == 0, side_x, side_y), sizes, across_diagonal)
    stacks = [here, side_x, side_y, corner]
    return stacks + [shift(stack, sizes, across_core) for stack in stacks]


def scatter_sums(sums, sizes, core_me):
    depth = sizes[0]
    mine = sums[0] + shift(sums[1], sizes, across_core)
    corner = shift(mine[1, 1], sizes, across_diagonal)
    side_x = mine[0, 1] + jnp.where(core_me == 0, corner, 0.0)
    side_y = mine[1, 0] + jnp.where(core_me == 0, 0.0, corner)
    here = mine[0, 0] + shift(side_x, sizes, across_x) + shift(side_y, sizes, across_y)
    total = here[0]
    for step in range(1, depth):
        total = total + shift(here[step], sizes, lambda z, x, y, c, step=step: (z - step, x, y, c))
    return total


def gathered(
    density,
    factors,
    orthogonalizers,
    slot_pairs,
    density_source,
    density_column,
    target_row,
    target_column,
):
    tiles_all = lax.axis_size("tile")
    aux_count = lax.axis_size("aux")
    tile_me = lax.axis_index("tile")
    aux_me = lax.axis_index("aux")
    tile_width = factors.shape[-1]
    task_count = slot_pairs.shape[0]
    per_block = tiles_all // aux_count
    sizes = grid_of(tiles_all, aux_count)
    depth = sizes[0]
    z_me, x_me = tile_me // 2, tile_me % 2
    y_me, core_me = aux_me // 2, aux_me % 2

    split_factors = prep(factors)
    stacks = gather_shards(density, sizes, core_me)

    start = (tile_me * aux_count + aux_me) * task_count

    def own(table):
        return lax.dynamic_slice_in_dim(table[:, 0], start, task_count)

    def place(row, column, sign):
        aux = column // per_block
        dz = (sign * (z_me - row // 2)) % depth
        dx = (row % 2 + x_me) % 2
        dy = (aux // 2 + y_me) % 2
        dc = (aux % 2 + core_me) % 2
        return ((dc * 2 + dy) * 2 + dx) * depth + dz, column % per_block

    source, column = own(density_source), own(density_column)
    row_a, col_b = own(target_row), own(target_column)
    table = jnp.stack(
        [slot_pairs[:, 0], slot_pairs[:, 1], *place(source, column, 1), *place(row_a, col_b, 1), *place(col_b, row_a, 1)]
    )
    sums = run_tasks(table, split_factors, stacks)
    sums = sums.reshape((2, 2, 2, depth) + density.shape)
    symmetric = scatter_sums(sums, sizes, core_me)

    blocks_x = orthogonalizers.reshape(tiles_all, tile_width, tile_width)
    left_x = blocks_x[tile_me]
    right_x = lax.dynamic_slice_in_dim(blocks_x, aux_me * per_block, per_block, 0)
    leftward = jnp.einsum("ki,kn->in", left_x, symmetric, precision=highest)
    leftward = leftward.reshape(tile_width, per_block, tile_width)
    fock = jnp.einsum("ibl,blj->ibj", leftward, right_x, precision=highest)
    return fock.reshape(tile_width, per_block * tile_width)


def local(density, *rest):
    tiles_all = lax.axis_size("tile")
    aux_count = lax.axis_size("aux")
    whole = density.size * density.dtype.itemsize * tiles_all * aux_count
    pairs = tiles_all % 2 == 0 and aux_count == 4 and tiles_all % aux_count == 0
    if pairs and whole <= GATHER_LIMIT:
        return gathered(density, *rest)
    return routed(density, *rest)


def solution(mesh):
    return jax.shard_map(
        local,
        mesh=mesh,
        in_specs=(
            P("tile", "aux"),
            P(("tile", "aux"), None, None, None),
            P(),
            P(("tile", "aux"), None),
            P(),
            P(),
            P(),
            P(),
        ),
        out_specs=P("tile", "aux"),
        check_vma=False,
    )
```

```python
import functools

import jax
import jax.numpy as jnp
from jax import lax
from jax.experimental import pallas as pl
from jax.experimental.pallas import tpu as pltpu
from jax.sharding import PartitionSpec as P


highest = lax.Precision.HIGHEST
AXES = ("tile", "aux")
GATHER_LIMIT = 16 << 20


def ranks_of(key_rows):
    task_count = key_rows.shape[-1]
    position = jnp.arange(task_count)
    earlier = position[None, :] < position[:, None]
    matching = key_rows[..., :, None] == key_rows[..., None, :]
    return jnp.sum(matching & earlier, axis=-1)


def slot_table(key_rows, other_rows, wanted, capacity):
    ranking = ranks_of(key_rows)
    levels = jnp.arange(capacity)
    chosen = (key_rows == wanted)[..., None, :] & (ranking[..., None, :] == levels[:, None])
    picked = jnp.sum(jnp.where(chosen, other_rows[..., None, :], 0), axis=-1)
    filled = jnp.any(chosen, axis=-1)
    return (picked, filled)


def routed(
    density,
    factors,
    orthogonalizers,
    slot_pairs,
    density_source,
    density_column,
    target_row,
    target_column,
):
    tiles_all = lax.axis_size("tile")
    aux_count = lax.axis_size("aux")
    tile_me = lax.axis_index("tile")
    aux_me = lax.axis_index("aux")
    tile_width = factors.shape[-1]
    task_count = slot_pairs.shape[0]
    capacity = max(2, 2 * task_count // tiles_all)
    quarter = tile_width // aux_count
    per_block = tiles_all // aux_count
    source_grid = density_source.reshape(tiles_all, aux_count, task_count)
    column_grid = density_column.reshape(tiles_all, aux_count, task_count)
    target_grid = target_row.reshape(tiles_all, aux_count, task_count)
    target_cols = target_column.reshape(tiles_all, aux_count, task_count)
    own_source = source_grid[tile_me, aux_me]
    own_target = target_grid[tile_me, aux_me]
    row_slab = lax.all_gather(density, "aux", axis=1, tiled=True)
    slab_tiles = row_slab.reshape(tile_width, tiles_all, tile_width)
    group_source = lax.dynamic_index_in_dim(source_grid, aux_me, 1, False)
    group_column = lax.dynamic_index_in_dim(column_grid, aux_me, 1, False)
    send_cols, send_filled = slot_table(group_source, group_column, tile_me, capacity)
    outgoing = jnp.take(slab_tiles, send_cols, axis=1)
    outgoing = jnp.where(send_filled[None, :, :, None], outgoing, 0.0)
    incoming = lax.all_to_all(outgoing, "tile", split_axis=1, concat_axis=1, tiled=True)
    own_rank = ranks_of(own_source)
    group = 8
    batches = task_count // group

    def one_batch(items):
        sources, rank_block, lefts, rights = items
        dens_block = incoming[:, sources, rank_block, :]
        halfway = jnp.einsum("gpik,kgl->gpil", factors[lefts], dens_block, precision=highest)
        return jnp.einsum("gpil,gplj->gij", halfway, factors[rights], precision=highest)

    partials = lax.map(
        one_batch,
        (
            own_source.reshape(batches, group),
            own_rank.reshape(batches, group),
            slot_pairs[:, 0].reshape(batches, group),
            slot_pairs[:, 1].reshape(batches, group),
        ),
    )
    partials = partials.reshape(task_count, tile_width, tile_width)
    task_ids = jnp.arange(task_count, dtype=jnp.int32)
    owners = jnp.arange(tiles_all, dtype=jnp.int32)[:, None]
    send_task, send_live = slot_table(own_target[None, :], task_ids[None, :], owners, capacity)
    outbound = jnp.where(send_live[:, :, None, None], partials[send_task], 0.0)
    arrived = lax.all_to_all(outbound, "tile", split_axis=0, concat_axis=0, tiled=True)
    group_target = lax.dynamic_index_in_dim(target_grid, aux_me, 1, False)
    group_cols = lax.dynamic_index_in_dim(target_cols, aux_me, 1, False)
    cols_b, cols_live = slot_table(group_target, group_cols, tile_me, capacity)
    spread = ((cols_b.reshape(-1)[None, :] == owners) & cols_live.reshape(-1)[None, :]).astype(
        jnp.float32
    )
    row_sums = jnp.einsum(
        "bs,sij->ibj", spread, arrived.reshape(-1, tile_width, tile_width), precision=highest
    )
    row_sums = row_sums.reshape(tile_width, tiles_all * tile_width)
    exchange_rows = lax.psum_scatter(row_sums, "aux", scatter_dimension=0, tiled=True)
    mirrored = lax.all_to_all(
        lax.all_to_all(
            exchange_rows.reshape(quarter, tiles_all, tile_width),
            "tile",
            split_axis=1,
            concat_axis=1,
            tiled=True,
        ),
        "aux",
        split_axis=1,
        concat_axis=0,
        tiled=True,
    )
    full_rows = lax.all_to_all(
        exchange_rows.reshape(quarter, aux_count, per_block * tile_width),
        "aux",
        split_axis=1,
        concat_axis=0,
        tiled=True,
    )
    direct_part = full_rows.reshape(tile_width, per_block, tile_width)
    symmetric = direct_part + jnp.transpose(mirrored, (2, 1, 0))
    blocks_x = orthogonalizers.reshape(tiles_all, tile_width, tile_width)
    left_x = blocks_x[tile_me]
    right_x = lax.dynamic_slice_in_dim(blocks_x, aux_me * per_block, per_block, 0)
    leftward = jnp.einsum("ki,kbl->ibl", left_x, symmetric, precision=highest)
    fock = jnp.einsum("ibl,blj->ibj", leftward, right_x, precision=highest)
    return fock.reshape(tile_width, per_block * tile_width)


MIB = 1 << 20
UNROLL = 4
ROW_STAGE, ROW_LEFT, ROW_RIGHT, ROW_SHARD, ROW_PART, ROW_A, ROW_AC, ROW_B, ROW_BC = range(9)


def split(x):
    hi = x.astype(jnp.bfloat16)
    lo = (x - hi.astype(jnp.float32)).astype(jnp.bfloat16)
    return hi, lo


def prep_kernel(f_hbm, o_ref, buf, sem):
    slots, rows, w = f_hbm.shape
    copies = [pltpu.make_async_copy(f_hbm.at[s], buf.at[s], sem.at[s]) for s in range(slots)]
    for copy in copies:
        copy.start()
    step = 256
    for s, copy in enumerate(copies):
        copy.wait()

        @pl.loop(0, rows // step)
        def _(i, s=s):
            at = pl.ds(pl.multiple_of(i * step, step), step)
            hi, lo = split(buf[s, at, :])
            o_ref[s, at, :w] = hi
            o_ref[s, at, w:] = lo


def prep(factors):
    s, p, w, _ = factors.shape
    rows = p * w
    return pl.pallas_call(
        prep_kernel,
        in_specs=[pl.BlockSpec(memory_space=pl.ANY)],
        out_specs=pl.BlockSpec(memory_space=pltpu.VMEM),
        out_shape=jax.ShapeDtypeStruct((s, rows, 2 * w), jnp.bfloat16),
        scratch_shapes=[pltpu.VMEM((s, rows, w), jnp.float32), pltpu.SemaphoreType.DMA((s,))],
        compiler_params=pltpu.CompilerParams(vmem_limit_bytes=16 * MIB),
        cost_estimate=pl.CostEstimate(flops=2 * factors.size, bytes_accessed=8 * factors.size, transcendentals=0),
    )(factors.reshape(s, rows, w))


def task_kernel(stage, first, firsts, cuts, tab, *refs):
    f2, *refs = refs
    if not first:
        sums_in, *refs = refs
    stacks, refs = refs[: len(firsts)], refs[len(firsts) :]
    outs, (sums, order, tiles, sem) = refs[: len(refs) - 4], refs[len(refs) - 4 :]
    w = f2.shape[2] // 2
    tasks = tab.shape[1]
    pairs = f2.shape[1] // (2 * w)
    f32 = jnp.float32

    def pick(q, count):
        mine = tab[ROW_STAGE, q] == stage

        @pl.when(mine)
        def _():
            order[count] = q
            shard, part = tab[ROW_SHARD, q], pl.multiple_of(tab[ROW_PART, q] * w, w)
            for start, stack in zip(firsts, stacks):
                @pl.when((shard >= start) & (shard < start + stack.shape[0]))
                def _(start=start, stack=stack):
                    pltpu.make_async_copy(
                        stack.at[shard - start, :, pl.ds(part, w)], tiles.at[count], sem.at[count]
                    ).start()

        return count + mine.astype(jnp.int32)

    count = lax.fori_loop(0, tasks, pick, 0)
    sums[...] = jnp.zeros_like(sums) if first else sums_in[...]

    def rows(p):
        return slice(p * 2 * w, (p + 1) * 2 * w)

    def one(i):
        q = order[i]
        left, right = tab[ROW_LEFT, q], tab[ROW_RIGHT, q]
        hi, lo = split(tiles[i])
        half = jnp.concatenate([hi, lo], axis=1)
        wt = jnp.concatenate([half, half], axis=0)
        acc = None
        for p in range(pairs):
            h = jnp.dot(f2[left, rows(p), :], wt, preferred_element_type=f32)
            hi, lo = split(h[:, :w] + h[:, w:])
            lhs = jnp.concatenate(
                [jnp.concatenate([hi[:w], hi[w:]], axis=1), jnp.concatenate([lo[:w], lo[w:]], axis=1)], axis=0
            )
            d = jnp.dot(lhs, f2[right, rows(p), :], preferred_element_type=f32)
            acc = d if acc is None else acc + d
        part = acc[:w] + acc[w:]
        part = part[:, :w] + part[:, w:]
        c = pl.ds(pl.multiple_of(tab[ROW_AC, q] * w, w), w)
        sums[tab[ROW_A, q], :, c] = sums[tab[ROW_A, q], :, c] + part
        c = pl.ds(pl.multiple_of(tab[ROW_BC, q] * w, w), w)
        sums[tab[ROW_B, q], :, c] = sums[tab[ROW_B, q], :, c] + part.T

    def several(start, n):
        for k in range(n):
            pltpu.make_async_copy(stacks[0].at[0, :, pl.ds(0, w)], tiles.at[start + k], sem.at[start + k]).wait()
        for k in range(n):
            one(start + k)

    def many(i, carry):
        several(i * UNROLL, UNROLL)
        return carry

    def single(i, carry):
        several(i, 1)
        return carry

    lax.fori_loop(0, count // UNROLL, many, 0)
    lax.fori_loop(count // UNROLL * UNROLL, count, single, 0)
    if cuts:
        for start, out in zip(cuts, outs):
            out[...] = sums[start : start + out.shape[0]]


def run_stage(table, stage, f2, stacks, firsts, sums, shape, cuts=()):
    tasks = table.shape[1]
    w = f2.shape[2] // 2
    first = sums is None
    vmem = pl.BlockSpec(memory_space=pltpu.VMEM)
    ends = list(cuts[1:]) + [shape[0]]
    shapes = [(end - start,) + shape[1:] for start, end in zip(cuts, ends)] if cuts else [shape]
    outs = [jax.ShapeDtypeStruct(s, jnp.float32) for s in shapes]
    kept = [pltpu.VMEM(shape, jnp.float32)] if cuts else []
    body = functools.partial(task_kernel, stage, first, tuple(firsts), tuple(cuts))
    return pl.pallas_call(
        body,
        in_specs=[pl.BlockSpec(memory_space=pltpu.SMEM)] + [vmem] * (1 if first else 2)
        + [pl.BlockSpec(memory_space=pl.ANY)] * len(stacks),
        out_specs=[vmem] * len(outs),
        out_shape=outs,
        scratch_shapes=kept + [
            pltpu.SMEM((tasks,), jnp.int32),
            pltpu.VMEM((tasks, w, w), jnp.float32),
            pltpu.SemaphoreType.DMA((tasks,)),
        ],
        compiler_params=pltpu.CompilerParams(vmem_limit_bytes=20 * MIB),
        cost_estimate=pl.CostEstimate(flops=tasks * f2.shape[1] * w * w * 4, bytes_accessed=2 * f2.size, transcendentals=0),
    )(table, f2, *([] if first else [sums]), *stacks)


def shift(value, sizes, move):
    depth, wide, tall, cores = sizes
    pairs = []
    for source in range(depth * wide * tall * cores):
        rest, c = divmod(source, cores)
        rest, y = divmod(rest, tall)
        z, x = divmod(rest, wide)
        tz, tx, ty, tc = move(z, x, y, c)
        pairs.append((source, (((tz % depth) * wide + tx) * tall + ty) * cores + tc))
    return lax.ppermute(value, AXES, pairs)


def across_x(z, x, y, c):
    return z, 1 - x, y, c


def across_y(z, x, y, c):
    return z, x, 1 - y, c


def across_core(z, x, y, c):
    return z, x, y, 1 - c


def across_diagonal(z, x, y, c):
    return (z, x, 1 - y, c) if c == 0 else (z, 1 - x, y, c)


def across_z(step):
    return lambda z, x, y, c: (z + step, x, y, c)


def gathered(
    density,
    factors,
    orthogonalizers,
    slot_pairs,
    density_source,
    density_column,
    target_row,
    target_column,
):
    tiles_all = lax.axis_size("tile")
    aux_count = lax.axis_size("aux")
    tile_me = lax.axis_index("tile")
    aux_me = lax.axis_index("aux")
    tile_width = factors.shape[-1]
    task_count = slot_pairs.shape[0]
    per_block = tiles_all // aux_count
    depth = tiles_all // 2
    far = depth - 1
    sizes = (depth, 2, aux_count // 2, 2)
    z_me, x_me = tile_me // 2, tile_me % 2
    y_me, core_me = aux_me // 2, aux_me % 2
    on_first = core_me == 0

    def move(value, how):
        return shift(value, sizes, how)

    start = (tile_me * aux_count + aux_me) * task_count

    def own(table):
        return lax.dynamic_slice_in_dim(table[:, 0], start, task_count)

    def place(row, column, sign):
        aux = column // per_block
        dz = (sign * (z_me - row // 2)) & (depth - 1) if depth & far == 0 else (sign * (z_me - row // 2)) % depth
        side = ((aux // 2) ^ y_me) * 2 + ((row & 1) ^ x_me)
        shard = ((aux & 1) ^ core_me) * 4 * depth + jnp.where(dz == 0, side, 3 + side * far + dz)
        stage = jnp.where((dz == 0) | (side == 0), 0, jnp.where(side == 3, 2, 1))
        return stage, shard, column % per_block

    row_a, col_b = own(target_row), own(target_column)
    stage, source, part = place(own(density_source), own(density_column), 1)
    _, shard_a, part_a = place(row_a, col_b, 1)
    _, shard_b, part_b = place(col_b, row_a, 1)
    table = jnp.stack([stage, slot_pairs[:, 0], slot_pairs[:, 1], source, part, shard_a, part_a, shard_b, part_b])

    column = [move(density, across_z(step)) for step in range(1, depth)]
    near_x, near_y = move(density, across_x), move(density, across_y)
    near_d = move(jnp.where(on_first, near_x, near_y), across_diagonal)
    near = jnp.stack([density, near_x, near_y, near_d])
    near_c = move(near, across_core)
    split_factors = prep(factors)
    column, split_factors, table = lax.optimization_barrier((jnp.stack(column), split_factors, table))
    column_c = move(column, across_core)
    side_x = move(column, across_x)
    side_y = move(column, across_y)
    corner = move(jnp.where(on_first, side_x, side_y), across_diagonal)
    side_xc, side_yc, corner_c = (move(value, across_core) for value in (side_x, side_y, corner))

    firsts = [0, 4, 4 + far, 4 + 2 * far, 4 + 3 * far]
    other = [first + 4 * depth for first in firsts]
    shape = (8 * depth,) + density.shape
    (sums,) = run_stage(
        table, 0, split_factors, [near, near_c, column, column_c], [firsts[0], other[0], firsts[1], other[1]], None, shape
    )
    (sums,) = run_stage(
        table, 1, split_factors, [side_x, side_y, side_xc, side_yc], firsts[2:4] + other[2:4], sums, shape
    )
    mine_and_others = run_stage(
        table, 2, split_factors, [corner, corner_c], [firsts[4], other[4]], sums, shape, firsts + other
    )
    mine, others = mine_and_others[:5], mine_and_others[5:]

    corner = mine[4] + move(others[4], across_core)
    near = mine[0] + move(others[0], across_core)
    corner_in = move(corner, across_diagonal)
    near_in = move(near[3], across_diagonal)
    side_x = mine[2] + move(others[2], across_core)
    side_y = mine[3] + move(others[3], across_core)
    column = mine[1] + move(others[1], across_core)
    side_x = side_x + jnp.where(on_first, corner_in, 0.0)
    side_y = side_y + jnp.where(on_first, 0.0, corner_in)
    near_x = near[1] + jnp.where(on_first, near_in, 0.0)
    near_y = near[2] + jnp.where(on_first, 0.0, near_in)
    column = column + move(side_x, across_x) + move(side_y, across_y)
    total = near[0] + move(near_x, across_x) + move(near_y, across_y)
    for step in range(1, depth):
        total = total + move(column[step - 1], across_z(-step))

    blocks_x = orthogonalizers.reshape(tiles_all, tile_width, tile_width)
    left_x = blocks_x[tile_me]
    right_x = lax.dynamic_slice_in_dim(blocks_x, aux_me * per_block, per_block, 0)
    leftward = jnp.einsum("ki,kn->in", left_x, total, precision=highest)
    leftward = leftward.reshape(tile_width, per_block, tile_width)
    fock = jnp.einsum("ibl,blj->ibj", leftward, right_x, precision=highest)
    return fock.reshape(tile_width, per_block * tile_width)


def local(density, *rest):
    tiles_all = lax.axis_size("tile")
    aux_count = lax.axis_size("aux")
    whole = density.size * density.dtype.itemsize * tiles_all * aux_count
    pairs = tiles_all % 2 == 0 and aux_count == 4 and tiles_all % aux_count == 0
    if pairs and whole <= GATHER_LIMIT:
        return gathered(density, *rest)
    return routed(density, *rest)


def solution(mesh):
    return jax.shard_map(
        local,
        mesh=mesh,
        in_specs=(
            P("tile", "aux"),
            P(("tile", "aux"), None, None, None),
            P(),
            P(("tile", "aux"), None),
            P(),
            P(),
            P(),
            P(),
        ),
        out_specs=P("tile", "aux"),
        check_vma=False,
    )
```

```python
import functools

import jax
import jax.numpy as jnp
from jax import lax
from jax.experimental import pallas as pl
from jax.experimental.pallas import tpu as pltpu
from jax.sharding import PartitionSpec as P


highest = lax.Precision.HIGHEST
AXES = ("tile", "aux")
GATHER_LIMIT = 16 << 20


def ranks_of(key_rows):
    task_count = key_rows.shape[-1]
    position = jnp.arange(task_count)
    earlier = position[None, :] < position[:, None]
    matching = key_rows[..., :, None] == key_rows[..., None, :]
    return jnp.sum(matching & earlier, axis=-1)


def slot_table(key_rows, other_rows, wanted, capacity):
    ranking = ranks_of(key_rows)
    levels = jnp.arange(capacity)
    chosen = (key_rows == wanted)[..., None, :] & (ranking[..., None, :] == levels[:, None])
    picked = jnp.sum(jnp.where(chosen, other_rows[..., None, :], 0), axis=-1)
    filled = jnp.any(chosen, axis=-1)
    return (picked, filled)


def routed(
    density,
    factors,
    orthogonalizers,
    slot_pairs,
    density_source,
    density_column,
    target_row,
    target_column,
):
    tiles_all = lax.axis_size("tile")
    aux_count = lax.axis_size("aux")
    tile_me = lax.axis_index("tile")
    aux_me = lax.axis_index("aux")
    tile_width = factors.shape[-1]
    task_count = slot_pairs.shape[0]
    capacity = max(2, 2 * task_count // tiles_all)
    quarter = tile_width // aux_count
    per_block = tiles_all // aux_count
    source_grid = density_source.reshape(tiles_all, aux_count, task_count)
    column_grid = density_column.reshape(tiles_all, aux_count, task_count)
    target_grid = target_row.reshape(tiles_all, aux_count, task_count)
    target_cols = target_column.reshape(tiles_all, aux_count, task_count)
    own_source = source_grid[tile_me, aux_me]
    own_target = target_grid[tile_me, aux_me]
    row_slab = lax.all_gather(density, "aux", axis=1, tiled=True)
    slab_tiles = row_slab.reshape(tile_width, tiles_all, tile_width)
    group_source = lax.dynamic_index_in_dim(source_grid, aux_me, 1, False)
    group_column = lax.dynamic_index_in_dim(column_grid, aux_me, 1, False)
    send_cols, send_filled = slot_table(group_source, group_column, tile_me, capacity)
    outgoing = jnp.take(slab_tiles, send_cols, axis=1)
    outgoing = jnp.where(send_filled[None, :, :, None], outgoing, 0.0)
    incoming = lax.all_to_all(outgoing, "tile", split_axis=1, concat_axis=1, tiled=True)
    own_rank = ranks_of(own_source)
    group = 8
    batches = task_count // group

    def one_batch(items):
        sources, rank_block, lefts, rights = items
        dens_block = incoming[:, sources, rank_block, :]
        halfway = jnp.einsum("gpik,kgl->gpil", factors[lefts], dens_block, precision=highest)
        return jnp.einsum("gpil,gplj->gij", halfway, factors[rights], precision=highest)

    partials = lax.map(
        one_batch,
        (
            own_source.reshape(batches, group),
            own_rank.reshape(batches, group),
            slot_pairs[:, 0].reshape(batches, group),
            slot_pairs[:, 1].reshape(batches, group),
        ),
    )
    partials = partials.reshape(task_count, tile_width, tile_width)
    task_ids = jnp.arange(task_count, dtype=jnp.int32)
    owners = jnp.arange(tiles_all, dtype=jnp.int32)[:, None]
    send_task, send_live = slot_table(own_target[None, :], task_ids[None, :], owners, capacity)
    outbound = jnp.where(send_live[:, :, None, None], partials[send_task], 0.0)
    arrived = lax.all_to_all(outbound, "tile", split_axis=0, concat_axis=0, tiled=True)
    group_target = lax.dynamic_index_in_dim(target_grid, aux_me, 1, False)
    group_cols = lax.dynamic_index_in_dim(target_cols, aux_me, 1, False)
    cols_b, cols_live = slot_table(group_target, group_cols, tile_me, capacity)
    spread = ((cols_b.reshape(-1)[None, :] == owners) & cols_live.reshape(-1)[None, :]).astype(
        jnp.float32
    )
    row_sums = jnp.einsum(
        "bs,sij->ibj", spread, arrived.reshape(-1, tile_width, tile_width), precision=highest
    )
    row_sums = row_sums.reshape(tile_width, tiles_all * tile_width)
    exchange_rows = lax.psum_scatter(row_sums, "aux", scatter_dimension=0, tiled=True)
    mirrored = lax.all_to_all(
        lax.all_to_all(
            exchange_rows.reshape(quarter, tiles_all, tile_width),
            "tile",
            split_axis=1,
            concat_axis=1,
            tiled=True,
        ),
        "aux",
        split_axis=1,
        concat_axis=0,
        tiled=True,
    )
    full_rows = lax.all_to_all(
        exchange_rows.reshape(quarter, aux_count, per_block * tile_width),
        "aux",
        split_axis=1,
        concat_axis=0,
        tiled=True,
    )
    direct_part = full_rows.reshape(tile_width, per_block, tile_width)
    symmetric = direct_part + jnp.transpose(mirrored, (2, 1, 0))
    blocks_x = orthogonalizers.reshape(tiles_all, tile_width, tile_width)
    left_x = blocks_x[tile_me]
    right_x = lax.dynamic_slice_in_dim(blocks_x, aux_me * per_block, per_block, 0)
    leftward = jnp.einsum("ki,kbl->ibl", left_x, symmetric, precision=highest)
    fock = jnp.einsum("ibl,blj->ibj", leftward, right_x, precision=highest)
    return fock.reshape(tile_width, per_block * tile_width)


MIB = 1 << 20
UNROLL = 4
ROW_STAGE, ROW_SHARD, ROW_PART, ROW_LEFT, ROW_RIGHT, ROW_A, ROW_AC, ROW_B, ROW_BC = range(9)


def split(x):
    hi = x.astype(jnp.bfloat16)
    lo = (x - hi.astype(jnp.float32)).astype(jnp.bfloat16)
    return hi, lo


def prep_kernel(f_hbm, o_ref, buf, sem):
    slots, rows, w = f_hbm.shape
    copies = [pltpu.make_async_copy(f_hbm.at[s], buf.at[s], sem.at[s]) for s in range(slots)]
    for copy in copies:
        copy.start()
    step = 256
    for s, copy in enumerate(copies):
        copy.wait()

        @pl.loop(0, rows // step)
        def _(i, s=s):
            at = pl.ds(pl.multiple_of(i * step, step), step)
            hi, lo = split(buf[s, at, :])
            o_ref[s, at, :w] = hi
            o_ref[s, at, w:] = lo


def prep(factors):
    s, p, w, _ = factors.shape
    rows = p * w
    return pl.pallas_call(
        prep_kernel,
        in_specs=[pl.BlockSpec(memory_space=pltpu.HBM)],
        out_specs=pl.BlockSpec(memory_space=pltpu.VMEM),
        out_shape=jax.ShapeDtypeStruct((s, rows, 2 * w), jnp.bfloat16),
        scratch_shapes=[pltpu.VMEM((s, rows, w), jnp.float32), pltpu.SemaphoreType.DMA((s,))],
        compiler_params=pltpu.CompilerParams(vmem_limit_bytes=8 * MIB),
        cost_estimate=pl.CostEstimate(flops=2 * factors.size, bytes_accessed=8 * factors.size, transcendentals=0),
    )(pltpu.with_memory_space_constraint(factors.reshape(s, rows, w), pltpu.HBM))


def task_kernel(stage, first, firsts, cuts, tab, *refs):
    f2, *refs = refs
    if not first:
        sums_in, *refs = refs
    stacks, refs = refs[: len(firsts)], refs[len(firsts) :]
    outs, (sums, order, tiles, sem) = refs[: len(refs) - 4], refs[len(refs) - 4 :]
    w = f2.shape[2] // 2
    tasks = tab.shape[1]
    pairs = f2.shape[1] // (2 * w)
    f32 = jnp.float32

    def pick(q, count):
        mine = tab[ROW_STAGE, q] == stage

        @pl.when(mine)
        def _():
            order[count] = q
            shard, part = tab[ROW_SHARD, q], pl.multiple_of(tab[ROW_PART, q] * w, w)
            for start, stack in zip(firsts, stacks):
                @pl.when((shard >= start) & (shard < start + stack.shape[0]))
                def _(start=start, stack=stack):
                    pltpu.make_async_copy(
                        stack.at[shard - start, :, pl.ds(part, w)], tiles.at[count], sem.at[count]
                    ).start()

        return count + mine.astype(jnp.int32)

    count = lax.fori_loop(0, tasks, pick, 0)
    sums[...] = jnp.zeros_like(sums) if first else sums_in[...]

    def rows(p):
        return slice(p * 2 * w, (p + 1) * 2 * w)

    def one(i):
        q = order[i]
        left, right = tab[ROW_LEFT, q], tab[ROW_RIGHT, q]
        hi, lo = split(tiles[i])
        half = jnp.concatenate([hi, lo], axis=1)
        wt = jnp.concatenate([half, half], axis=0)
        acc = None
        for p in range(pairs):
            h = jnp.dot(f2[left, rows(p), :], wt, preferred_element_type=f32)
            hi, lo = split(h[:, :w] + h[:, w:])
            lhs = jnp.concatenate(
                [jnp.concatenate([hi[:w], hi[w:]], axis=1), jnp.concatenate([lo[:w], lo[w:]], axis=1)], axis=0
            )
            d = jnp.dot(lhs, f2[right, rows(p), :], preferred_element_type=f32)
            acc = d if acc is None else acc + d
        part = acc[:w] + acc[w:]
        part = part[:, :w] + part[:, w:]
        c = pl.ds(pl.multiple_of(tab[ROW_AC, q] * w, w), w)
        sums[tab[ROW_A, q], :, c] = sums[tab[ROW_A, q], :, c] + part
        c = pl.ds(pl.multiple_of(tab[ROW_BC, q] * w, w), w)
        sums[tab[ROW_B, q], :, c] = sums[tab[ROW_B, q], :, c] + part.T

    def several(start, n):
        for k in range(n):
            pltpu.make_async_copy(stacks[0].at[0, :, pl.ds(0, w)], tiles.at[start + k], sem.at[start + k]).wait()
        for k in range(n):
            one(start + k)

    def many(i, carry):
        several(i * UNROLL, UNROLL)
        return carry

    def single(i, carry):
        several(i, 1)
        return carry

    lax.fori_loop(0, count // UNROLL, many, 0)
    done = count // UNROLL * UNROLL

    @pl.when(count - done >= 2)
    def _():
        several(done, 2)

    lax.fori_loop(count // 2 * 2, count, single, 0)
    if cuts:
        for start, out in zip(cuts, outs):
            out[...] = sums[start : start + out.shape[0]]


def run_stage(table, stage, f2, stacks, firsts, sums, shape, cuts=()):
    tasks = table.shape[1]
    w = f2.shape[2] // 2
    first = sums is None
    vmem = pl.BlockSpec(memory_space=pltpu.VMEM)
    ends = list(cuts[1:]) + [shape[0]]
    shapes = [(end - start,) + shape[1:] for start, end in zip(cuts, ends)] if cuts else [shape]
    outs = [jax.ShapeDtypeStruct(s, jnp.float32) for s in shapes]
    kept = [pltpu.VMEM(shape, jnp.float32)] if cuts else []
    body = functools.partial(task_kernel, stage, first, tuple(firsts), tuple(cuts))
    return pl.pallas_call(
        body,
        in_specs=[pl.BlockSpec(memory_space=pltpu.SMEM)] + [vmem] * (1 if first else 2)
        + [pl.BlockSpec(memory_space=pl.ANY)] * len(stacks),
        out_specs=[vmem] * len(outs),
        out_shape=outs,
        scratch_shapes=kept + [
            pltpu.SMEM((tasks,), jnp.int32),
            pltpu.VMEM((tasks, w, w), jnp.float32),
            pltpu.SemaphoreType.DMA((tasks,)),
        ],
        compiler_params=pltpu.CompilerParams(vmem_limit_bytes=12 * MIB),
        cost_estimate=pl.CostEstimate(flops=tasks * f2.shape[1] * w * w * 4, bytes_accessed=2 * f2.size, transcendentals=0),
    )(table, f2, *([] if first else [sums]), *stacks)


def shift(value, sizes, move):
    depth, wide, tall, cores = sizes
    pairs = []
    for source in range(depth * wide * tall * cores):
        rest, c = divmod(source, cores)
        rest, y = divmod(rest, tall)
        z, x = divmod(rest, wide)
        tz, tx, ty, tc = move(z, x, y, c)
        pairs.append((source, (((tz % depth) * wide + tx) * tall + ty) * cores + tc))
    return lax.ppermute(value, AXES, pairs)


def across_x(z, x, y, c):
    return z, 1 - x, y, c


def across_y(z, x, y, c):
    return z, x, 1 - y, c


def across_core(z, x, y, c):
    return z, x, y, 1 - c


def across_diagonal(z, x, y, c):
    return (z, x, 1 - y, c) if c == 0 else (z, 1 - x, y, c)


def across_z(step):
    return lambda z, x, y, c: (z ^ step, x, y, c)


def gathered(
    density,
    factors,
    orthogonalizers,
    slot_pairs,
    density_source,
    density_column,
    target_row,
    target_column,
):
    tiles_all = lax.axis_size("tile")
    aux_count = lax.axis_size("aux")
    tile_me = lax.axis_index("tile")
    aux_me = lax.axis_index("aux")
    tile_width = factors.shape[-1]
    task_count = slot_pairs.shape[0]
    per_block = tiles_all // aux_count
    depth = tiles_all // 2
    chunks = depth // 2
    sizes = (depth, 2, aux_count // 2, 2)
    z_me, x_me = tile_me >> 1, tile_me & 1
    y_me, core_me = aux_me >> 1, aux_me & 1
    on_first = core_me == 0

    def move(value, how):
        return shift(value, sizes, how)

    start = (tile_me * aux_count + aux_me) * task_count

    def own(table):
        return lax.dynamic_slice_in_dim(table[:, 0], start, task_count)

    def place(row, column):
        aux = column // per_block
        side = ((aux >> 1) ^ y_me) * 2 + ((row & 1) ^ x_me)
        return (aux & 1) ^ core_me, (row >> 1) ^ z_me, side, column % per_block

    def source_of(row, column):
        dc, dz, side, part = place(row, column)
        stage = jnp.where(side > 0, 1, 0) + jnp.where(side == 3, 1, 0) + jnp.where(dz > 1, 1, 0)
        return stage, ((dc * chunks + (dz >> 1)) * 4 + side) * 2 + (dz & 1), part

    def target_of(row, column):
        dc, dz, side, part = place(row, column)
        turn = (chunks - 1 - (dz >> 1)) * 2
        straight = jnp.where(side == 0, 3 * depth, 0) + turn + (dz & 1)
        sideways = depth + turn * 2 + (side - 1) * 2 + (dz & 1)
        at = jnp.where((side == 1) | (side == 2), sideways, straight)
        return dc * 4 * depth + at, part

    row_a, col_b = own(target_row), own(target_column)
    rows = [
        *source_of(own(density_source), own(density_column)),
        slot_pairs[:, 0],
        slot_pairs[:, 1],
        *target_of(row_a, col_b),
        *target_of(col_b, row_a),
    ]
    which = lax.broadcasted_iota(jnp.int32, (len(rows), task_count), 0)
    table = sum(jnp.where(which == at, row[None, :], 0) for at, row in enumerate(rows))

    column = [density] + [move(density, across_z(step)) for step in range(1, depth)]
    split_factors = prep(factors)
    by_stage = [([], []) for _ in range(4)]
    for k in range(chunks):
        here = jnp.stack(column[2 * k : 2 * k + 2])
        if k == 0:
            here, split_factors, on_first = lax.optimization_barrier((here, split_factors, on_first))
        side_x = move(here, across_x)
        side_y = move(here, across_y)
        corner = move(jnp.where(on_first, side_x, side_y), across_diagonal)
        for side, value in enumerate((here, side_x, side_y, corner)):
            stage = min(side, 1) + (side == 3) + (k > 0)
            first = (k * 4 + side) * 2
            for at, stack in ((first, value), (first + 4 * depth, move(value, across_core))):
                by_stage[stage][0].append(stack)
                by_stage[stage][1].append(at)

    shape = (8 * depth,) + density.shape
    groups = [0, depth] + [depth + 4 * k for k in range(1, chunks)] + [3 * depth]
    sums = None
    for stage, (values, firsts) in enumerate(by_stage):
        cuts = groups + [4 * depth + at for at in groups] if stage == 3 else ()
        results = run_stage(table, stage, split_factors, values, firsts, sums, shape, cuts)
        sums = results[0]
    mine, others = results[: len(groups)], results[len(groups) :]

    merged = [a + move(b, across_core) for a, b in zip(mine, others)]
    column = merged[-1]
    total = None
    corners = []
    for turn in range(chunks):
        corners.append(move(merged[0][2 * turn : 2 * turn + 2], across_diagonal))
    for turn in range(chunks):
        sides = merged[1 + turn]
        side_x = sides[:2] + jnp.where(on_first, corners[turn], 0.0)
        side_y = sides[2:] + jnp.where(on_first, 0.0, corners[turn])
        here = column[2 * turn : 2 * turn + 2]
        here = here + move(side_x, across_x) + move(side_y, across_y)
        for bit in range(2):
            step = (chunks - 1 - turn) * 2 + bit
            value = move(here[bit], across_z(step)) if step else here[bit]
            total = value if total is None else total + value

    blocks_x = orthogonalizers.reshape(tiles_all, tile_width, tile_width)
    left_x = blocks_x[tile_me]
    right_x = lax.dynamic_slice_in_dim(blocks_x, aux_me * per_block, per_block, 0)
    leftward = jnp.einsum("ki,kn->in", left_x, total, precision=highest)
    leftward = leftward.reshape(tile_width, per_block, tile_width)
    fock = jnp.einsum("ibl,blj->ibj", leftward, right_x, precision=highest)
    return fock.reshape(tile_width, per_block * tile_width)


def local(density, *rest):
    tiles_all = lax.axis_size("tile")
    aux_count = lax.axis_size("aux")
    whole = density.size * density.dtype.itemsize * tiles_all * aux_count
    cube = aux_count == 4 and tiles_all >= aux_count and tiles_all & (tiles_all - 1) == 0
    if cube and whole <= GATHER_LIMIT:
        return gathered(density, *rest)
    return routed(density, *rest)


def solution(mesh):
    return jax.shard_map(
        local,
        mesh=mesh,
        in_specs=(
            P("tile", "aux"),
            P(("tile", "aux"), None, None, None),
            P(),
            P(("tile", "aux"), None),
            P(),
            P(),
            P(),
            P(),
        ),
        out_specs=P("tile", "aux"),
        check_vma=False,
    )
```

```python
import functools

import jax
import jax.numpy as jnp
from jax import lax
from jax.experimental import pallas as pl
from jax.experimental.pallas import tpu as pltpu
from jax.sharding import PartitionSpec as P


highest = lax.Precision.HIGHEST
AXES = ("tile", "aux")
GATHER_LIMIT = 16 << 20


def ranks_of(key_rows):
    task_count = key_rows.shape[-1]
    position = jnp.arange(task_count)
    earlier = position[None, :] < position[:, None]
    matching = key_rows[..., :, None] == key_rows[..., None, :]
    return jnp.sum(matching & earlier, axis=-1)


def slot_table(key_rows, other_rows, wanted, capacity):
    ranking = ranks_of(key_rows)
    levels = jnp.arange(capacity)
    chosen = (key_rows == wanted)[..., None, :] & (ranking[..., None, :] == levels[:, None])
    picked = jnp.sum(jnp.where(chosen, other_rows[..., None, :], 0), axis=-1)
    filled = jnp.any(chosen, axis=-1)
    return (picked, filled)


def routed(
    density,
    factors,
    orthogonalizers,
    slot_pairs,
    density_source,
    density_column,
    target_row,
    target_column,
):
    tiles_all = lax.axis_size("tile")
    aux_count = lax.axis_size("aux")
    tile_me = lax.axis_index("tile")
    aux_me = lax.axis_index("aux")
    tile_width = factors.shape[-1]
    task_count = slot_pairs.shape[0]
    capacity = max(2, 2 * task_count // tiles_all)
    quarter = tile_width // aux_count
    per_block = tiles_all // aux_count
    source_grid = density_source.reshape(tiles_all, aux_count, task_count)
    column_grid = density_column.reshape(tiles_all, aux_count, task_count)
    target_grid = target_row.reshape(tiles_all, aux_count, task_count)
    target_cols = target_column.reshape(tiles_all, aux_count, task_count)
    own_source = source_grid[tile_me, aux_me]
    own_target = target_grid[tile_me, aux_me]
    row_slab = lax.all_gather(density, "aux", axis=1, tiled=True)
    slab_tiles = row_slab.reshape(tile_width, tiles_all, tile_width)
    group_source = lax.dynamic_index_in_dim(source_grid, aux_me, 1, False)
    group_column = lax.dynamic_index_in_dim(column_grid, aux_me, 1, False)
    send_cols, send_filled = slot_table(group_source, group_column, tile_me, capacity)
    outgoing = jnp.take(slab_tiles, send_cols, axis=1)
    outgoing = jnp.where(send_filled[None, :, :, None], outgoing, 0.0)
    incoming = lax.all_to_all(outgoing, "tile", split_axis=1, concat_axis=1, tiled=True)
    own_rank = ranks_of(own_source)
    group = 8
    batches = task_count // group

    def one_batch(items):
        sources, rank_block, lefts, rights = items
        dens_block = incoming[:, sources, rank_block, :]
        halfway = jnp.einsum("gpik,kgl->gpil", factors[lefts], dens_block, precision=highest)
        return jnp.einsum("gpil,gplj->gij", halfway, factors[rights], precision=highest)

    partials = lax.map(
        one_batch,
        (
            own_source.reshape(batches, group),
            own_rank.reshape(batches, group),
            slot_pairs[:, 0].reshape(batches, group),
            slot_pairs[:, 1].reshape(batches, group),
        ),
    )
    partials = partials.reshape(task_count, tile_width, tile_width)
    task_ids = jnp.arange(task_count, dtype=jnp.int32)
    owners = jnp.arange(tiles_all, dtype=jnp.int32)[:, None]
    send_task, send_live = slot_table(own_target[None, :], task_ids[None, :], owners, capacity)
    outbound = jnp.where(send_live[:, :, None, None], partials[send_task], 0.0)
    arrived = lax.all_to_all(outbound, "tile", split_axis=0, concat_axis=0, tiled=True)
    group_target = lax.dynamic_index_in_dim(target_grid, aux_me, 1, False)
    group_cols = lax.dynamic_index_in_dim(target_cols, aux_me, 1, False)
    cols_b, cols_live = slot_table(group_target, group_cols, tile_me, capacity)
    spread = ((cols_b.reshape(-1)[None, :] == owners) & cols_live.reshape(-1)[None, :]).astype(
        jnp.float32
    )
    row_sums = jnp.einsum(
        "bs,sij->ibj", spread, arrived.reshape(-1, tile_width, tile_width), precision=highest
    )
    row_sums = row_sums.reshape(tile_width, tiles_all * tile_width)
    exchange_rows = lax.psum_scatter(row_sums, "aux", scatter_dimension=0, tiled=True)
    mirrored = lax.all_to_all(
        lax.all_to_all(
            exchange_rows.reshape(quarter, tiles_all, tile_width),
            "tile",
            split_axis=1,
            concat_axis=1,
            tiled=True,
        ),
        "aux",
        split_axis=1,
        concat_axis=0,
        tiled=True,
    )
    full_rows = lax.all_to_all(
        exchange_rows.reshape(quarter, aux_count, per_block * tile_width),
        "aux",
        split_axis=1,
        concat_axis=0,
        tiled=True,
    )
    direct_part = full_rows.reshape(tile_width, per_block, tile_width)
    symmetric = direct_part + jnp.transpose(mirrored, (2, 1, 0))
    blocks_x = orthogonalizers.reshape(tiles_all, tile_width, tile_width)
    left_x = blocks_x[tile_me]
    right_x = lax.dynamic_slice_in_dim(blocks_x, aux_me * per_block, per_block, 0)
    leftward = jnp.einsum("ki,kbl->ibl", left_x, symmetric, precision=highest)
    fock = jnp.einsum("ibl,blj->ibj", leftward, right_x, precision=highest)
    return fock.reshape(tile_width, per_block * tile_width)


MIB = 1 << 20
UNROLL = 4
ROW_STAGE, ROW_SHARD, ROW_PART, ROW_LEFT, ROW_RIGHT, ROW_A, ROW_AC, ROW_B, ROW_BC = range(9)


def split(x):
    hi = x.astype(jnp.bfloat16)
    lo = (x - hi.astype(jnp.float32)).astype(jnp.bfloat16)
    return hi, lo


def prep_kernel(f_hbm, o_ref, buf, sem):
    slots, rows, w = f_hbm.shape
    copies = [pltpu.make_async_copy(f_hbm.at[s], buf.at[s], sem.at[s]) for s in range(slots)]
    for copy in copies:
        copy.start()
    step = 256
    for s, copy in enumerate(copies):
        copy.wait()

        @pl.loop(0, rows // step)
        def _(i, s=s):
            at = pl.ds(pl.multiple_of(i * step, step), step)
            hi, lo = split(buf[s, at, :])
            o_ref[s, at, :w] = hi
            o_ref[s, at, w:] = lo


def prep(factors):
    s, p, w, _ = factors.shape
    rows = p * w
    return pl.pallas_call(
        prep_kernel,
        in_specs=[pl.BlockSpec(memory_space=pltpu.HBM)],
        out_specs=pl.BlockSpec(memory_space=pltpu.VMEM),
        out_shape=jax.ShapeDtypeStruct((s, rows, 2 * w), jnp.bfloat16),
        scratch_shapes=[pltpu.VMEM((s, rows, w), jnp.float32), pltpu.SemaphoreType.DMA((s,))],
        compiler_params=pltpu.CompilerParams(vmem_limit_bytes=8 * MIB),
        cost_estimate=pl.CostEstimate(flops=2 * factors.size, bytes_accessed=8 * factors.size, transcendentals=0),
    )(pltpu.with_memory_space_constraint(factors.reshape(s, rows, w), pltpu.HBM))


def task_kernel(stage, first, keep, firsts, cuts, tab, *refs):
    f2, *refs = refs
    if not first:
        sums_in, *refs = refs
    stacks, refs = refs[: len(firsts)], refs[len(firsts) :]
    if keep:
        sums, *refs = refs
    outs, refs = refs[: len(cuts)], refs[len(cuts) :]
    if not keep:
        sums, *refs = refs
    order, tiles, sem = refs
    w = f2.shape[2] // 2
    tasks = tab.shape[1]
    pairs = f2.shape[1] // (2 * w)
    f32 = jnp.float32

    def pick(q, count):
        mine = tab[ROW_STAGE, q] == stage

        @pl.when(mine)
        def _():
            order[count] = q
            shard, part = tab[ROW_SHARD, q], pl.multiple_of(tab[ROW_PART, q] * w, w)
            for start, stack in zip(firsts, stacks):
                @pl.when((shard >= start) & (shard < start + stack.shape[0]))
                def _(start=start, stack=stack):
                    pltpu.make_async_copy(
                        stack.at[shard - start, :, pl.ds(part, w)], tiles.at[count], sem.at[count]
                    ).start()

        return count + mine.astype(jnp.int32)

    count = lax.fori_loop(0, tasks, pick, 0)
    sums[...] = jnp.zeros_like(sums) if first else sums_in[...]

    def rows(p):
        return slice(p * 2 * w, (p + 1) * 2 * w)

    def one(i):
        q = order[i]
        left, right = tab[ROW_LEFT, q], tab[ROW_RIGHT, q]
        hi, lo = split(tiles[i])
        half = jnp.concatenate([hi, lo], axis=1)
        wt = jnp.concatenate([half, half], axis=0)
        acc = None
        for p in range(pairs):
            h = jnp.dot(f2[left, rows(p), :], wt, preferred_element_type=f32)
            hi, lo = split(h[:, :w] + h[:, w:])
            lhs = jnp.concatenate(
                [jnp.concatenate([hi[:w], hi[w:]], axis=1), jnp.concatenate([lo[:w], lo[w:]], axis=1)], axis=0
            )
            d = jnp.dot(lhs, f2[right, rows(p), :], preferred_element_type=f32)
            acc = d if acc is None else acc + d
        part = acc[:w] + acc[w:]
        part = part[:, :w] + part[:, w:]
        c = pl.ds(pl.multiple_of(tab[ROW_AC, q] * w, w), w)
        sums[tab[ROW_A, q], :, c] = sums[tab[ROW_A, q], :, c] + part
        c = pl.ds(pl.multiple_of(tab[ROW_BC, q] * w, w), w)
        sums[tab[ROW_B, q], :, c] = sums[tab[ROW_B, q], :, c] + part.T

    def several(start, n):
        for k in range(n):
            pltpu.make_async_copy(stacks[0].at[0, :, pl.ds(0, w)], tiles.at[start + k], sem.at[start + k]).wait()
        for k in range(n):
            one(start + k)

    def many(i, carry):
        several(i * UNROLL, UNROLL)
        return carry

    def single(i, carry):
        several(i, 1)
        return carry

    lax.fori_loop(0, count // UNROLL, many, 0)
    done = count // UNROLL * UNROLL

    @pl.when(count - done >= 2)
    def _():
        several(done, 2)

    lax.fori_loop(count // 2 * 2, count, single, 0)
    for (start, size), out in zip(cuts, outs):
        out[...] = sums[start : start + size]


def run_stage(table, stage, f2, stacks, firsts, sums, shape, cuts, keep):
    tasks = table.shape[1]
    w = f2.shape[2] // 2
    first = sums is None
    vmem = pl.BlockSpec(memory_space=pltpu.VMEM)
    shapes = ([shape] if keep else []) + [(size,) + shape[1:] for _, size in cuts]
    outs = [jax.ShapeDtypeStruct(s, jnp.float32) for s in shapes]
    body = functools.partial(task_kernel, stage, first, keep, tuple(firsts), tuple(cuts))
    return pl.pallas_call(
        body,
        in_specs=[pl.BlockSpec(memory_space=pltpu.SMEM)] + [vmem] * (1 if first else 2)
        + [pl.BlockSpec(memory_space=pl.ANY)] * len(stacks),
        out_specs=[vmem] * len(outs),
        out_shape=outs,
        scratch_shapes=([] if keep else [pltpu.VMEM(shape, jnp.float32)]) + [
            pltpu.SMEM((tasks,), jnp.int32),
            pltpu.VMEM((tasks, w, w), jnp.float32),
            pltpu.SemaphoreType.DMA((tasks,)),
        ],
        compiler_params=pltpu.CompilerParams(vmem_limit_bytes=12 * MIB),
        cost_estimate=pl.CostEstimate(flops=tasks * f2.shape[1] * w * w * 4, bytes_accessed=2 * f2.size, transcendentals=0),
    )(table, f2, *([] if first else [sums]), *stacks)


def shift(value, sizes, move):
    depth, wide, tall, cores = sizes
    pairs = []
    for source in range(depth * wide * tall * cores):
        rest, c = divmod(source, cores)
        rest, y = divmod(rest, tall)
        z, x = divmod(rest, wide)
        tz, tx, ty, tc = move(z, x, y, c)
        pairs.append((source, (((tz % depth) * wide + tx) * tall + ty) * cores + tc))
    return lax.ppermute(value, AXES, pairs)


def across_x(z, x, y, c):
    return z, 1 - x, y, c


def across_y(z, x, y, c):
    return z, x, 1 - y, c


def across_core(z, x, y, c):
    return z, x, y, 1 - c


def across_diagonal(z, x, y, c):
    return (z, x, 1 - y, c) if c == 0 else (z, 1 - x, y, c)


def across_z(step):
    return lambda z, x, y, c: (z ^ step, x, y, c)


def gathered(
    density,
    factors,
    orthogonalizers,
    slot_pairs,
    density_source,
    density_column,
    target_row,
    target_column,
):
    tiles_all = lax.axis_size("tile")
    aux_count = lax.axis_size("aux")
    tile_me = lax.axis_index("tile")
    aux_me = lax.axis_index("aux")
    tile_width = factors.shape[-1]
    task_count = slot_pairs.shape[0]
    per_block = tiles_all // aux_count
    depth = tiles_all // 2
    chunks = depth // 2
    sizes = (depth, 2, aux_count // 2, 2)
    z_me, x_me = tile_me >> 1, tile_me & 1
    y_me, core_me = aux_me >> 1, aux_me & 1
    on_first = core_me == 0

    def move(value, how):
        return shift(value, sizes, how)

    start = (tile_me * aux_count + aux_me) * task_count

    def own(table):
        return lax.dynamic_slice_in_dim(table[:, 0], start, task_count)

    def place(row, column):
        aux = column // per_block
        side = ((aux >> 1) ^ y_me) * 2 + ((row & 1) ^ x_me)
        return (aux & 1) ^ core_me, (row >> 1) ^ z_me, side, column % per_block

    def source_of(row, column):
        dc, dz, side, part = place(row, column)
        stage = jnp.where(side > 0, 1, 0) + jnp.where(side == 3, 1, 0) + jnp.where(dz > 1, 1, 0)
        return stage, ((dc * chunks + (dz >> 1)) * 4 + side) * 2 + (dz & 1), part

    def target_of(row, column):
        dc, dz, side, part = place(row, column)
        turn = (chunks - 1 - (dz >> 1)) * 2
        straight = jnp.where(side == 0, 3 * depth, 0) + turn + (dz & 1)
        sideways = depth + turn * 2 + (side - 1) * 2 + (dz & 1)
        at = jnp.where((side == 1) | (side == 2), sideways, straight)
        return side == 3, dc * 4 * depth + at, part

    row_a, col_b = own(target_row), own(target_column)
    corner_a, *target_a = target_of(row_a, col_b)
    corner_b, *target_b = target_of(col_b, row_a)
    stage, *source = source_of(own(density_source), own(density_column))
    stage = jnp.where((stage > 1) & ~(corner_a | corner_b), 4, stage)
    rows = [stage, *source, slot_pairs[:, 0], slot_pairs[:, 1], *target_a, *target_b]
    which = lax.broadcasted_iota(jnp.int32, (len(rows), task_count), 0)
    table = sum(jnp.where(which == at, row[None, :], 0) for at, row in enumerate(rows))

    column = [density] + [move(density, across_z(step)) for step in range(1, depth)]
    split_factors = prep(factors)
    by_stage = [([], []) for _ in range(4)]
    for k in range(chunks):
        here = jnp.stack(column[2 * k : 2 * k + 2])
        if k == 0:
            here, split_factors, on_first = lax.optimization_barrier((here, split_factors, on_first))
        side_x = move(here, across_x)
        side_y = move(here, across_y)
        corner = move(jnp.where(on_first, side_x, side_y), across_diagonal)
        for side, value in enumerate((here, side_x, side_y, corner)):
            stage = min(side, 1) + (side == 3) + (k > 0)
            first = (k * 4 + side) * 2
            for at, stack in ((first, value), (first + 4 * depth, move(value, across_core))):
                by_stage[stage][0].append(stack)
                by_stage[stage][1].append(at)

    by_stage.append(tuple(one + other for one, other in zip(by_stage[2], by_stage[3])))
    shape = (8 * depth,) + density.shape
    corner_cuts = [(at, depth) for at in (0, 4 * depth)]
    groups = [(depth + 4 * k, 4) for k in range(chunks)] + [(3 * depth + 2 * k, 2) for k in range(chunks)]
    cuts = groups + [(4 * depth + at, size) for at, size in groups]
    sums = None
    for stage, (values, firsts) in enumerate(by_stage):
        cut = {3: corner_cuts, 4: cuts}.get(stage, ())
        results = run_stage(table, stage, split_factors, values, firsts, sums, shape, cut, stage < 4)
        sums = results[0]
        if stage == 3:
            corner_mine, corner_other = results[1:]
    mine, others = results[: len(groups)], results[len(groups) :]

    corner = corner_mine + move(corner_other, across_core)
    merged = [a + move(b, across_core) for a, b in zip(mine, others)]
    corners = [move(corner[2 * k : 2 * k + 2], across_diagonal) for k in range(chunks)]
    total = None
    for k in range(chunks):
        sides, here = merged[k], merged[chunks + k]
        side_x = sides[:2] + jnp.where(on_first, corners[k], 0.0)
        side_y = sides[2:] + jnp.where(on_first, 0.0, corners[k])
        here = here + move(side_x, across_x) + move(side_y, across_y)
        for bit in range(2):
            step = (chunks - 1 - k) * 2 + bit
            value = move(here[bit], across_z(step)) if step else here[bit]
            total = value if total is None else total + value

    blocks_x = orthogonalizers.reshape(tiles_all, tile_width, tile_width)
    left_x = blocks_x[tile_me]
    right_x = lax.dynamic_slice_in_dim(blocks_x, aux_me * per_block, per_block, 0)
    leftward = jnp.einsum("ki,kn->in", left_x, total, precision=highest)
    leftward = leftward.reshape(tile_width, per_block, tile_width)
    fock = jnp.einsum("ibl,blj->ibj", leftward, right_x, precision=highest)
    return fock.reshape(tile_width, per_block * tile_width)


def local(density, *rest):
    tiles_all = lax.axis_size("tile")
    aux_count = lax.axis_size("aux")
    whole = density.size * density.dtype.itemsize * tiles_all * aux_count
    cube = aux_count == 4 and tiles_all >= aux_count and tiles_all & (tiles_all - 1) == 0
    if cube and whole <= GATHER_LIMIT:
        return gathered(density, *rest)
    return routed(density, *rest)


def solution(mesh):
    return jax.shard_map(
        local,
        mesh=mesh,
        in_specs=(
            P("tile", "aux"),
            P(("tile", "aux"), None, None, None),
            P(),
            P(("tile", "aux"), None),
            P(),
            P(),
            P(),
            P(),
        ),
        out_specs=P("tile", "aux"),
        check_vma=False,
    )
```

```python
import functools

import jax
import jax.numpy as jnp
from jax import lax
from jax.experimental import pallas as pl
from jax.experimental.pallas import tpu as pltpu
from jax.sharding import PartitionSpec as P


highest = lax.Precision.HIGHEST
AXES = ("tile", "aux")
GATHER_LIMIT = 16 << 20


def ranks_of(key_rows):
    task_count = key_rows.shape[-1]
    position = jnp.arange(task_count)
    earlier = position[None, :] < position[:, None]
    matching = key_rows[..., :, None] == key_rows[..., None, :]
    return jnp.sum(matching & earlier, axis=-1)


def slot_table(key_rows, other_rows, wanted, capacity):
    ranking = ranks_of(key_rows)
    levels = jnp.arange(capacity)
    chosen = (key_rows == wanted)[..., None, :] & (ranking[..., None, :] == levels[:, None])
    picked = jnp.sum(jnp.where(chosen, other_rows[..., None, :], 0), axis=-1)
    filled = jnp.any(chosen, axis=-1)
    return (picked, filled)


def routed(
    density,
    factors,
    orthogonalizers,
    slot_pairs,
    density_source,
    density_column,
    target_row,
    target_column,
):
    tiles_all = lax.axis_size("tile")
    aux_count = lax.axis_size("aux")
    tile_me = lax.axis_index("tile")
    aux_me = lax.axis_index("aux")
    tile_width = factors.shape[-1]
    task_count = slot_pairs.shape[0]
    capacity = max(2, 2 * task_count // tiles_all)
    quarter = tile_width // aux_count
    per_block = tiles_all // aux_count
    source_grid = density_source.reshape(tiles_all, aux_count, task_count)
    column_grid = density_column.reshape(tiles_all, aux_count, task_count)
    target_grid = target_row.reshape(tiles_all, aux_count, task_count)
    target_cols = target_column.reshape(tiles_all, aux_count, task_count)
    own_source = source_grid[tile_me, aux_me]
    own_target = target_grid[tile_me, aux_me]
    row_slab = lax.all_gather(density, "aux", axis=1, tiled=True)
    slab_tiles = row_slab.reshape(tile_width, tiles_all, tile_width)
    group_source = lax.dynamic_index_in_dim(source_grid, aux_me, 1, False)
    group_column = lax.dynamic_index_in_dim(column_grid, aux_me, 1, False)
    send_cols, send_filled = slot_table(group_source, group_column, tile_me, capacity)
    outgoing = jnp.take(slab_tiles, send_cols, axis=1)
    outgoing = jnp.where(send_filled[None, :, :, None], outgoing, 0.0)
    incoming = lax.all_to_all(outgoing, "tile", split_axis=1, concat_axis=1, tiled=True)
    own_rank = ranks_of(own_source)
    group = 8
    batches = task_count // group

    def one_batch(items):
        sources, rank_block, lefts, rights = items
        dens_block = incoming[:, sources, rank_block, :]
        halfway = jnp.einsum("gpik,kgl->gpil", factors[lefts], dens_block, precision=highest)
        return jnp.einsum("gpil,gplj->gij", halfway, factors[rights], precision=highest)

    partials = lax.map(
        one_batch,
        (
            own_source.reshape(batches, group),
            own_rank.reshape(batches, group),
            slot_pairs[:, 0].reshape(batches, group),
            slot_pairs[:, 1].reshape(batches, group),
        ),
    )
    partials = partials.reshape(task_count, tile_width, tile_width)
    task_ids = jnp.arange(task_count, dtype=jnp.int32)
    owners = jnp.arange(tiles_all, dtype=jnp.int32)[:, None]
    send_task, send_live = slot_table(own_target[None, :], task_ids[None, :], owners, capacity)
    outbound = jnp.where(send_live[:, :, None, None], partials[send_task], 0.0)
    arrived = lax.all_to_all(outbound, "tile", split_axis=0, concat_axis=0, tiled=True)
    group_target = lax.dynamic_index_in_dim(target_grid, aux_me, 1, False)
    group_cols = lax.dynamic_index_in_dim(target_cols, aux_me, 1, False)
    cols_b, cols_live = slot_table(group_target, group_cols, tile_me, capacity)
    spread = ((cols_b.reshape(-1)[None, :] == owners) & cols_live.reshape(-1)[None, :]).astype(
        jnp.float32
    )
    row_sums = jnp.einsum(
        "bs,sij->ibj", spread, arrived.reshape(-1, tile_width, tile_width), precision=highest
    )
    row_sums = row_sums.reshape(tile_width, tiles_all * tile_width)
    exchange_rows = lax.psum_scatter(row_sums, "aux", scatter_dimension=0, tiled=True)
    mirrored = lax.all_to_all(
        lax.all_to_all(
            exchange_rows.reshape(quarter, tiles_all, tile_width),
            "tile",
            split_axis=1,
            concat_axis=1,
            tiled=True,
        ),
        "aux",
        split_axis=1,
        concat_axis=0,
        tiled=True,
    )
    full_rows = lax.all_to_all(
        exchange_rows.reshape(quarter, aux_count, per_block * tile_width),
        "aux",
        split_axis=1,
        concat_axis=0,
        tiled=True,
    )
    direct_part = full_rows.reshape(tile_width, per_block, tile_width)
    symmetric = direct_part + jnp.transpose(mirrored, (2, 1, 0))
    blocks_x = orthogonalizers.reshape(tiles_all, tile_width, tile_width)
    left_x = blocks_x[tile_me]
    right_x = lax.dynamic_slice_in_dim(blocks_x, aux_me * per_block, per_block, 0)
    leftward = jnp.einsum("ki,kbl->ibl", left_x, symmetric, precision=highest)
    fock = jnp.einsum("ibl,blj->ibj", leftward, right_x, precision=highest)
    return fock.reshape(tile_width, per_block * tile_width)


MIB = 1 << 20
UNROLL = 4
STAGES = 5
FIELDS = 8
LEFT, RIGHT, STACK, PART, ROW_A, PART_A, ROW_B, PART_B = range(FIELDS)


def split(x):
    hi = x.astype(jnp.bfloat16)
    lo = (x - hi.astype(jnp.float32)).astype(jnp.bfloat16)
    return hi, lo


def plan_tasks(depth, per_block, aux_count, source, column, row, target, pairs, info, plan):
    tasks = pairs.shape[1]
    chunks = depth // 2
    tile_me, aux_me = lax.axis_index("tile"), lax.axis_index("aux")
    z_me, x_me, y_me, c_me = tile_me >> 1, tile_me & 1, aux_me >> 1, aux_me & 1
    start = (tile_me * aux_count + aux_me) * tasks

    def place(a, b):
        aux = lax.div(b, per_block)
        side = (((aux >> 1) ^ y_me) << 1) | ((a & 1) ^ x_me)
        return (aux & 1) ^ c_me, (a >> 1) ^ z_me, side, lax.rem(b, per_block)

    def target_of(a, b):
        dc, dz, side, part = place(a, b)
        turn = (chunks - 1 - (dz >> 1)) * 2
        straight = jnp.where(side == 0, 3 * depth, 0) + turn + (dz & 1)
        sideways = depth + turn * 2 + (side - 1) * 2 + (dz & 1)
        at = jnp.where((side == 1) | (side == 2), sideways, straight)
        return side == 3, dc * 4 * depth + at, part

    def read(q, carry):
        at = start + q
        dc, dz, side, part = place(source[0, at], column[0, at])
        one = lambda test: jnp.where(test, 1, 0)
        corner_a, row_a, part_a = target_of(row[0, at], target[0, at])
        corner_b, row_b, part_b = target_of(target[0, at], row[0, at])
        stack = ((dc * chunks + (dz >> 1)) * 4 + side) * 2 + (dz & 1)
        for f, value in enumerate((pairs[0, q], pairs[1, q], stack, part, row_a, part_a, row_b, part_b)):
            info[f, q] = value
        info[FIELDS, q] = one(side > 0) + one(side == 3) + one(dz > 1)
        info[FIELDS + 1, q] = one(corner_a | corner_b)
        return carry

    lax.fori_loop(0, tasks, read, 0)
    for s in range(STAGES):
        plan[s, 0] = 0
    for urgent in (1, 0):
        def put(q, carry, urgent=urgent):
            @pl.when(info[FIELDS + 1, q] == urgent)
            def _():
                wave = info[FIELDS, q]
                late = jnp.maximum(wave, 2) if urgent else 4
                stage = jnp.where((wave <= 1) & (plan[1, 0] < tasks * 3 // 8), 1, late)
                stage = jnp.where((wave == 0) & (plan[0, 0] < tasks // 4), 0, stage)
                n = plan[stage, 0]
                plan[stage, 0] = n + 1
                for f in range(FIELDS):
                    plan[stage, (n + 1) * FIELDS + f] = info[f, q]

            return carry

        lax.fori_loop(0, tasks, put, 0)


def prepare_kernel(depth, per_block, aux_count, *refs):
    f_hbm, plan, o_ref, buf, info, sem = refs[5:]
    slots, rows, w = f_hbm.shape
    copies = [pltpu.make_async_copy(f_hbm.at[s], buf.at[s], sem.at[s]) for s in range(slots)]
    for copy in copies:
        copy.start()
    plan_tasks(depth, per_block, aux_count, *refs[:5], info, plan)
    step = 256
    for s, copy in enumerate(copies):
        copy.wait()

        @pl.loop(0, rows // step)
        def _(i, s=s):
            at = pl.ds(pl.multiple_of(i * step, step), step)
            hi, lo = split(buf[s, at, :])
            o_ref[s, at, :w] = hi
            o_ref[s, at, w:] = lo


def prepare(depth, per_block, aux_count, tables, pairs, factors):
    s, p, w, _ = factors.shape
    rows = p * w
    tasks = pairs.shape[0]
    smem = pl.BlockSpec(memory_space=pltpu.SMEM)
    return pl.pallas_call(
        functools.partial(prepare_kernel, depth, per_block, aux_count),
        in_specs=[smem] * 5 + [pl.BlockSpec(memory_space=pltpu.HBM)],
        out_specs=[smem, pl.BlockSpec(memory_space=pltpu.VMEM)],
        out_shape=[
            jax.ShapeDtypeStruct((STAGES, (tasks + 1) * FIELDS), jnp.int32),
            jax.ShapeDtypeStruct((s, rows, 2 * w), jnp.bfloat16),
        ],
        scratch_shapes=[
            pltpu.VMEM((s, rows, w), jnp.float32),
            pltpu.SMEM((FIELDS + 2, tasks), jnp.int32),
            pltpu.SemaphoreType.DMA((s,)),
        ],
        compiler_params=pltpu.CompilerParams(vmem_limit_bytes=8 * MIB),
        cost_estimate=pl.CostEstimate(flops=2 * factors.size, bytes_accessed=8 * factors.size, transcendentals=0),
    )(
        *(pltpu.with_memory_space_constraint(table.T, pltpu.HBM) for table in (*tables, pairs)),
        pltpu.with_memory_space_constraint(factors.reshape(s, rows, w), pltpu.HBM),
    )


def task_kernel(stage, first, keep, firsts, cuts, plan, *refs):
    f2, *refs = refs
    if not first:
        sums_in, *refs = refs
    stacks, refs = refs[: len(firsts)], refs[len(firsts) :]
    if keep:
        sums, *refs = refs
    outs, refs = refs[: len(cuts)], refs[len(cuts) :]
    if not keep:
        sums, *refs = refs
    tiles, sem = refs
    w = f2.shape[2] // 2
    pairs = f2.shape[1] // (2 * w)
    f32 = jnp.float32

    count = plan[stage, 0]

    def field(i, f):
        return plan[stage, (i + 1) * FIELDS + f]

    def fetch(i, carry):
        shard, part = field(i, STACK), pl.multiple_of(field(i, PART) * w, w)
        for start, stack in zip(firsts, stacks):
            @pl.when((shard >= start) & (shard < start + stack.shape[0]))
            def _(start=start, stack=stack):
                pltpu.make_async_copy(stack.at[shard - start, :, pl.ds(part, w)], tiles.at[i], sem.at[i]).start()

        return carry

    lax.fori_loop(0, count, fetch, 0)
    sums[...] = jnp.zeros_like(sums) if first else sums_in[...]

    def rows(p):
        return slice(p * 2 * w, (p + 1) * 2 * w)

    def one(i):
        left, right = field(i, LEFT), field(i, RIGHT)
        hi, lo = split(tiles[i])
        half = jnp.concatenate([hi, lo], axis=1)
        wt = jnp.concatenate([half, half], axis=0)
        acc = None
        for p in range(pairs):
            h = jnp.dot(f2[left, rows(p), :], wt, preferred_element_type=f32)
            hi, lo = split(h[:, :w] + h[:, w:])
            lhs = jnp.concatenate(
                [jnp.concatenate([hi[:w], hi[w:]], axis=1), jnp.concatenate([lo[:w], lo[w:]], axis=1)], axis=0
            )
            d = jnp.dot(lhs, f2[right, rows(p), :], preferred_element_type=f32)
            acc = d if acc is None else acc + d
        part = acc[:w] + acc[w:]
        part = part[:, :w] + part[:, w:]
        for row, column, value in ((ROW_A, PART_A, part), (ROW_B, PART_B, part.T)):
            at, c = field(i, row), pl.ds(pl.multiple_of(field(i, column) * w, w), w)
            sums[at, :, c] = sums[at, :, c] + value

    def several(start, n):
        for k in range(n):
            pltpu.make_async_copy(stacks[0].at[0, :, pl.ds(0, w)], tiles.at[start + k], sem.at[start + k]).wait()
        for k in range(n):
            one(start + k)

    def many(i, carry):
        several(i * UNROLL, UNROLL)
        return carry

    def single(i, carry):
        several(i, 1)
        return carry

    lax.fori_loop(0, count // UNROLL, many, 0)
    done = count // UNROLL * UNROLL

    @pl.when(count - done >= 2)
    def _():
        several(done, 2)

    lax.fori_loop(count // 2 * 2, count, single, 0)
    for (start, size), out in zip(cuts, outs):
        out[...] = sums[start : start + size]


def run_stage(plan, stage, f2, stacks, firsts, sums, shape, cuts, keep):
    tasks = plan.shape[1] // FIELDS - 1
    w = f2.shape[2] // 2
    first = sums is None
    vmem = pl.BlockSpec(memory_space=pltpu.VMEM)
    shapes = ([shape] if keep else []) + [(size,) + shape[1:] for _, size in cuts]
    outs = [jax.ShapeDtypeStruct(s, jnp.float32) for s in shapes]
    body = functools.partial(task_kernel, stage, first, keep, tuple(firsts), tuple(cuts))
    return pl.pallas_call(
        body,
        in_specs=[pl.BlockSpec(memory_space=pltpu.SMEM)] + [vmem] * (1 if first else 2)
        + [pl.BlockSpec(memory_space=pl.ANY)] * len(stacks),
        out_specs=[vmem] * len(outs),
        out_shape=outs,
        scratch_shapes=([] if keep else [pltpu.VMEM(shape, jnp.float32)]) + [
            pltpu.VMEM((tasks, w, w), jnp.float32),
            pltpu.SemaphoreType.DMA((tasks,)),
        ],
        compiler_params=pltpu.CompilerParams(vmem_limit_bytes=12 * MIB),
        cost_estimate=pl.CostEstimate(flops=tasks * f2.shape[1] * w * w * 4, bytes_accessed=2 * f2.size, transcendentals=0),
    )(plan, f2, *([] if first else [sums]), *stacks)


def shift(value, sizes, move):
    depth, wide, tall, cores = sizes
    pairs = []
    for source in range(depth * wide * tall * cores):
        rest, c = divmod(source, cores)
        rest, y = divmod(rest, tall)
        z, x = divmod(rest, wide)
        tz, tx, ty, tc = move(z, x, y, c)
        pairs.append((source, (((tz % depth) * wide + tx) * tall + ty) * cores + tc))
    return lax.ppermute(value, AXES, pairs)


def across_x(z, x, y, c):
    return z, 1 - x, y, c


def across_y(z, x, y, c):
    return z, x, 1 - y, c


def across_core(z, x, y, c):
    return z, x, y, 1 - c


def across_diagonal(z, x, y, c):
    return (z, x, 1 - y, c) if c == 0 else (z, 1 - x, y, c)


def across_z(step):
    return lambda z, x, y, c: (z ^ step, x, y, c)


def gathered(
    density,
    factors,
    orthogonalizers,
    slot_pairs,
    density_source,
    density_column,
    target_row,
    target_column,
):
    tiles_all = lax.axis_size("tile")
    aux_count = lax.axis_size("aux")
    tile_me = lax.axis_index("tile")
    aux_me = lax.axis_index("aux")
    tile_width = factors.shape[-1]
    per_block = tiles_all // aux_count
    depth = tiles_all // 2
    chunks = depth // 2
    sizes = (depth, 2, aux_count // 2, 2)
    on_first = (aux_me & 1) == 0

    def move(value, how):
        return shift(value, sizes, how)

    column = [density] + [move(density, across_z(step)) for step in range(1, depth)]
    tables = (density_source, density_column, target_row, target_column)
    plan, split_factors = prepare(depth, per_block, aux_count, tables, slot_pairs, factors)
    by_stage = [([], []) for _ in range(4)]
    for k in range(chunks):
        here = jnp.stack(column[2 * k : 2 * k + 2])
        if k == 0:
            here, split_factors, on_first = lax.optimization_barrier((here, split_factors, on_first))
        side_x = move(here, across_x)
        side_y = move(here, across_y)
        corner = move(jnp.where(on_first, side_x, side_y), across_diagonal)
        for side, value in enumerate((here, side_x, side_y, corner)):
            stage = min(side, 1) + (side == 3) + (k > 0)
            first = (k * 4 + side) * 2
            for at, stack in ((first, value), (first + 4 * depth, move(value, across_core))):
                by_stage[stage][0].append(stack)
                by_stage[stage][1].append(at)

    for known in range(2):
        by_stage[1][known].extend(by_stage[0][known])
        by_stage[2][known].extend(by_stage[1][known])
    by_stage.append(tuple(one + other for one, other in zip(by_stage[2], by_stage[3])))
    shape = (8 * depth,) + density.shape
    corner_cuts = [(at, depth) for at in (0, 4 * depth)]
    groups = [(depth + 4 * k, 4) for k in range(chunks)] + [(3 * depth + 2 * k, 2) for k in range(chunks)]
    cuts = groups + [(4 * depth + at, size) for at, size in groups]
    sums = None
    for stage, (values, firsts) in enumerate(by_stage):
        cut = {3: corner_cuts, 4: cuts}.get(stage, ())
        results = run_stage(plan, stage, split_factors, values, firsts, sums, shape, cut, stage < 4)
        sums = results[0]
        if stage == 3:
            corner_mine, corner_other = results[1:]
    mine, others = results[: len(groups)], results[len(groups) :]

    corner = corner_mine + move(corner_other, across_core)
    merged = [a + move(b, across_core) for a, b in zip(mine, others)]
    corners = [move(corner[2 * k : 2 * k + 2], across_diagonal) for k in range(chunks)]
    total = None
    for k in range(chunks):
        sides, here = merged[k], merged[chunks + k]
        side_x = sides[:2] + jnp.where(on_first, corners[k], 0.0)
        side_y = sides[2:] + jnp.where(on_first, 0.0, corners[k])
        here = here + move(side_x, across_x) + move(side_y, across_y)
        for bit in range(2):
            step = (chunks - 1 - k) * 2 + bit
            value = move(here[bit], across_z(step)) if step else here[bit]
            total = value if total is None else total + value

    blocks_x = orthogonalizers.reshape(tiles_all, tile_width, tile_width)
    left_x = blocks_x[tile_me]
    right_x = lax.dynamic_slice_in_dim(blocks_x, aux_me * per_block, per_block, 0)
    leftward = jnp.einsum("ki,kn->in", left_x, total, precision=highest)
    leftward = leftward.reshape(tile_width, per_block, tile_width)
    fock = jnp.einsum("ibl,blj->ibj", leftward, right_x, precision=highest)
    return fock.reshape(tile_width, per_block * tile_width)


def local(density, *rest):
    tiles_all = lax.axis_size("tile")
    aux_count = lax.axis_size("aux")
    whole = density.size * density.dtype.itemsize * tiles_all * aux_count
    cube = aux_count == 4 and tiles_all >= aux_count and tiles_all & (tiles_all - 1) == 0
    if cube and whole <= GATHER_LIMIT:
        return gathered(density, *rest)
    return routed(density, *rest)


def solution(mesh):
    return jax.shard_map(
        local,
        mesh=mesh,
        in_specs=(
            P("tile", "aux"),
            P(("tile", "aux"), None, None, None),
            P(),
            P(("tile", "aux"), None),
            P(),
            P(),
            P(),
            P(),
        ),
        out_specs=P("tile", "aux"),
        check_vma=False,
    )
```

```python
import functools

import jax
import jax.numpy as jnp
from jax import lax
from jax.experimental import pallas as pl
from jax.experimental.pallas import tpu as pltpu
from jax.sharding import PartitionSpec as P


highest = lax.Precision.HIGHEST
AXES = ("tile", "aux")
GATHER_LIMIT = 16 << 20


def ranks_of(key_rows):
    task_count = key_rows.shape[-1]
    position = jnp.arange(task_count)
    earlier = position[None, :] < position[:, None]
    matching = key_rows[..., :, None] == key_rows[..., None, :]
    return jnp.sum(matching & earlier, axis=-1)


def slot_table(key_rows, other_rows, wanted, capacity):
    ranking = ranks_of(key_rows)
    levels = jnp.arange(capacity)
    chosen = (key_rows == wanted)[..., None, :] & (ranking[..., None, :] == levels[:, None])
    picked = jnp.sum(jnp.where(chosen, other_rows[..., None, :], 0), axis=-1)
    filled = jnp.any(chosen, axis=-1)
    return (picked, filled)


def routed(
    density,
    factors,
    orthogonalizers,
    slot_pairs,
    density_source,
    density_column,
    target_row,
    target_column,
):
    tiles_all = lax.axis_size("tile")
    aux_count = lax.axis_size("aux")
    tile_me = lax.axis_index("tile")
    aux_me = lax.axis_index("aux")
    tile_width = factors.shape[-1]
    task_count = slot_pairs.shape[0]
    capacity = max(2, 2 * task_count // tiles_all)
    quarter = tile_width // aux_count
    per_block = tiles_all // aux_count
    source_grid = density_source.reshape(tiles_all, aux_count, task_count)
    column_grid = density_column.reshape(tiles_all, aux_count, task_count)
    target_grid = target_row.reshape(tiles_all, aux_count, task_count)
    target_cols = target_column.reshape(tiles_all, aux_count, task_count)
    own_source = source_grid[tile_me, aux_me]
    own_target = target_grid[tile_me, aux_me]
    row_slab = lax.all_gather(density, "aux", axis=1, tiled=True)
    slab_tiles = row_slab.reshape(tile_width, tiles_all, tile_width)
    group_source = lax.dynamic_index_in_dim(source_grid, aux_me, 1, False)
    group_column = lax.dynamic_index_in_dim(column_grid, aux_me, 1, False)
    send_cols, send_filled = slot_table(group_source, group_column, tile_me, capacity)
    outgoing = jnp.take(slab_tiles, send_cols, axis=1)
    outgoing = jnp.where(send_filled[None, :, :, None], outgoing, 0.0)
    incoming = lax.all_to_all(outgoing, "tile", split_axis=1, concat_axis=1, tiled=True)
    own_rank = ranks_of(own_source)
    group = 8
    batches = task_count // group

    def one_batch(items):
        sources, rank_block, lefts, rights = items
        dens_block = incoming[:, sources, rank_block, :]
        halfway = jnp.einsum("gpik,kgl->gpil", factors[lefts], dens_block, precision=highest)
        return jnp.einsum("gpil,gplj->gij", halfway, factors[rights], precision=highest)

    partials = lax.map(
        one_batch,
        (
            own_source.reshape(batches, group),
            own_rank.reshape(batches, group),
            slot_pairs[:, 0].reshape(batches, group),
            slot_pairs[:, 1].reshape(batches, group),
        ),
    )
    partials = partials.reshape(task_count, tile_width, tile_width)
    task_ids = jnp.arange(task_count, dtype=jnp.int32)
    owners = jnp.arange(tiles_all, dtype=jnp.int32)[:, None]
    send_task, send_live = slot_table(own_target[None, :], task_ids[None, :], owners, capacity)
    outbound = jnp.where(send_live[:, :, None, None], partials[send_task], 0.0)
    arrived = lax.all_to_all(outbound, "tile", split_axis=0, concat_axis=0, tiled=True)
    group_target = lax.dynamic_index_in_dim(target_grid, aux_me, 1, False)
    group_cols = lax.dynamic_index_in_dim(target_cols, aux_me, 1, False)
    cols_b, cols_live = slot_table(group_target, group_cols, tile_me, capacity)
    spread = ((cols_b.reshape(-1)[None, :] == owners) & cols_live.reshape(-1)[None, :]).astype(
        jnp.float32
    )
    row_sums = jnp.einsum(
        "bs,sij->ibj", spread, arrived.reshape(-1, tile_width, tile_width), precision=highest
    )
    row_sums = row_sums.reshape(tile_width, tiles_all * tile_width)
    exchange_rows = lax.psum_scatter(row_sums, "aux", scatter_dimension=0, tiled=True)
    mirrored = lax.all_to_all(
        lax.all_to_all(
            exchange_rows.reshape(quarter, tiles_all, tile_width),
            "tile",
            split_axis=1,
            concat_axis=1,
            tiled=True,
        ),
        "aux",
        split_axis=1,
        concat_axis=0,
        tiled=True,
    )
    full_rows = lax.all_to_all(
        exchange_rows.reshape(quarter, aux_count, per_block * tile_width),
        "aux",
        split_axis=1,
        concat_axis=0,
        tiled=True,
    )
    direct_part = full_rows.reshape(tile_width, per_block, tile_width)
    symmetric = direct_part + jnp.transpose(mirrored, (2, 1, 0))
    blocks_x = orthogonalizers.reshape(tiles_all, tile_width, tile_width)
    left_x = blocks_x[tile_me]
    right_x = lax.dynamic_slice_in_dim(blocks_x, aux_me * per_block, per_block, 0)
    leftward = jnp.einsum("ki,kbl->ibl", left_x, symmetric, precision=highest)
    fock = jnp.einsum("ibl,blj->ibj", leftward, right_x, precision=highest)
    return fock.reshape(tile_width, per_block * tile_width)


MIB = 1 << 20
UNROLL = 4
LANES = 128
STAGES = 5
FIELDS = 8
LEFT, RIGHT, STACK, PART, ROW_A, PART_A, ROW_B, PART_B = range(FIELDS)


def split(x):
    hi = x.astype(jnp.bfloat16)
    lo = (x - hi.astype(jnp.float32)).astype(jnp.bfloat16)
    return hi, lo


def waves_of(chunks):
    return [0, 2, 4 + 2 * chunks, 2 + 6 * chunks]


def plan_tasks(depth, per_block, aux_count, source, column, row, target, pairs, plan):
    tasks = pairs.shape[1]
    width = plan.shape[1]
    chunks = depth // 2
    begin = waves_of(chunks)
    tile_me, aux_me = lax.axis_index("tile"), lax.axis_index("aux")
    z_me, x_me, y_me, c_me = tile_me >> 1, tile_me & 1, aux_me >> 1, aux_me & 1
    start = (tile_me * aux_count + aux_me) * tasks
    where, f32 = jnp.where, jnp.float32

    def own(table):
        line = table[pl.ds(lax.div(start, LANES), 1), :]
        return pltpu.roll(line, lax.rem(LANES - lax.rem(start, LANES), LANES), 1)[:, :tasks]

    def place(a, b):
        aux = lax.div(b, jnp.full_like(b, per_block))
        side = (((aux >> 1) ^ y_me) << 1) | ((a & 1) ^ x_me)
        return (aux & 1) ^ c_me, (a >> 1) ^ z_me, side, b - aux * per_block

    def target_of(a, b):
        dc, dz, side, part = place(a, b)
        turn = (chunks - 1 - (dz >> 1)) * 2
        straight = where(side == 0, 3 * depth, 0) + turn + (dz & 1)
        sideways = depth + turn * 2 + (side - 1) * 2 + (dz & 1)
        at = where((side == 1) | (side == 2), sideways, straight)
        return where(side == 3, 1, 0), dc * 4 * depth + at, part

    dc, dz, side, part = place(own(source), own(column))
    far = dz >> 1
    near_at = where(side == 0, begin[0], where(side == 3, begin[2], 2 * side))
    far_at = where(side == 0, begin[1] + 2 + 2 * far, where(side == 3, begin[3] - 2 + 2 * far, begin[2] - 4 + 4 * far + 2 * side))
    stack = dc * 4 * depth + where(far == 0, near_at, far_at) + (dz & 1)
    wave = where(side > 0, 1, 0) + where(side == 3, 1, 0) + where(far > 0, 1, 0)
    a, b = own(row), own(target)
    corner_a, row_a, part_a = target_of(a, b)
    corner_b, row_b, part_b = target_of(b, a)
    urgent = corner_a | corner_b

    above = lax.broadcasted_iota(jnp.int32, (tasks, tasks), 0)
    along = lax.broadcasted_iota(jnp.int32, (tasks, tasks), 1)

    def upright(line):
        return jnp.sum(where(above == along, line.astype(f32), 0.0), axis=1, keepdims=True)

    place_in = lax.broadcasted_iota(jnp.int32, (1, tasks), 1)
    key = (place_in + (1 - urgent) * tasks).astype(f32)
    before = where(upright(key) < key, 1.0, 0.0)

    def rank(which):
        return jnp.sum(before * upright(which), axis=0, keepdims=True)

    first = where(wave == 0, 1, 0)
    first = where(rank(first) < tasks // 4, first, 0)
    second = where(wave <= 1, 1 - first, 0)
    second = where(rank(second) < tasks * 3 // 8, second, 0)
    late = where(urgent > 0, jnp.maximum(wave, 2), 4)
    stage = where(first > 0, 0, where(second > 0, 1, late))
    stage_up = upright(stage)
    earlier = where(above < along, 1.0, 0.0)
    turn = jnp.sum(where(stage_up == stage.astype(f32), earlier, 0.0), axis=0, keepdims=True)
    slot_up = upright(stage.astype(f32) * tasks + turn)
    slots = lax.broadcasted_iota(jnp.int32, (tasks, width), 1)
    slots = slots.astype(f32)
    chosen = where(slot_up == slots, 1.0, 0.0).astype(jnp.bfloat16)
    values = jnp.zeros((FIELDS, tasks), jnp.int32)
    lines = lax.broadcasted_iota(jnp.int32, (FIELDS, tasks), 0)
    for f, value in enumerate((pairs[0:1, :], pairs[1:2, :], stack, part, row_a, part_a, row_b, part_b)):
        values = where(lines == f, value, values)
    listed = jnp.dot(values.astype(f32).astype(jnp.bfloat16), chosen, preferred_element_type=f32)
    plan[:FIELDS, :] = listed.astype(jnp.int32)
    lowest = stage_up * tasks
    inside = where(lowest <= slots, 1.0, 0.0) * where(slots < lowest + tasks, 1.0, 0.0)
    counts = jnp.sum(inside, axis=0, keepdims=True)
    plan[FIELDS:, :] = jnp.broadcast_to(counts, (FIELDS, width)).astype(jnp.int32)


def prepare_kernel(depth, per_block, aux_count, *refs):
    f_hbm, plan, o_ref, buf, sem = refs[5:]
    slots, rows, w = f_hbm.shape
    copies = [pltpu.make_async_copy(f_hbm.at[s], buf.at[s], sem.at[s]) for s in range(slots)]
    for copy in copies:
        copy.start()
    plan_tasks(depth, per_block, aux_count, *refs[:5], plan)
    step = 256
    for s, copy in enumerate(copies):
        copy.wait()

        @pl.loop(0, rows // step)
        def _(i, s=s):
            at = pl.ds(pl.multiple_of(i * step, step), step)
            hi, lo = split(buf[s, at, :])
            o_ref[s, at, :w] = hi
            o_ref[s, at, w:] = lo


def prepare(depth, per_block, aux_count, tables, pairs, factors):
    s, p, w, _ = factors.shape
    rows = p * w
    tasks = pairs.shape[0]
    vmem = pl.BlockSpec(memory_space=pltpu.VMEM)
    width = -(-STAGES * tasks // LANES) * LANES
    return pl.pallas_call(
        functools.partial(prepare_kernel, depth, per_block, aux_count),
        in_specs=[vmem] * 5 + [pl.BlockSpec(memory_space=pltpu.HBM)],
        out_specs=[vmem, vmem],
        out_shape=[
            jax.ShapeDtypeStruct((2 * FIELDS, width), jnp.int32),
            jax.ShapeDtypeStruct((s, rows, 2 * w), jnp.bfloat16),
        ],
        scratch_shapes=[
            pltpu.VMEM((s, rows, w), jnp.float32),
            pltpu.SemaphoreType.DMA((s,)),
        ],
        compiler_params=pltpu.CompilerParams(vmem_limit_bytes=8 * MIB),
        cost_estimate=pl.CostEstimate(flops=2 * factors.size, bytes_accessed=8 * factors.size, transcendentals=0),
    )(
        *(pltpu.with_memory_space_constraint(table.reshape(-1, LANES), pltpu.HBM) for table in tables),
        pltpu.with_memory_space_constraint(pairs.T, pltpu.HBM),
        pltpu.with_memory_space_constraint(factors.reshape(s, rows, w), pltpu.HBM),
    )


def task_kernel(stage, first, keep, firsts, cuts, plan, *refs):
    f2, *refs = refs
    if not first:
        sums_in, *refs = refs
    stacks, refs = refs[: len(firsts)], refs[len(firsts) :]
    if keep:
        sums, *refs = refs
    outs, refs = refs[: len(cuts)], refs[len(cuts) :]
    if not keep:
        sums, *refs = refs
    tiles, sem = refs
    w = f2.shape[2] // 2
    pairs = f2.shape[1] // (2 * w)
    f32 = jnp.float32

    tasks = tiles.shape[0]
    count = plan[FIELDS, stage * tasks]

    def field(i, f):
        return plan[f, stage * tasks + i]

    def fetch(i, carry):
        shard, part = field(i, STACK), pl.multiple_of(field(i, PART) * w, w)
        for start, stack in zip(firsts, stacks):
            @pl.when((shard >= start) & (shard < start + stack.shape[0]))
            def _(start=start, stack=stack):
                pltpu.make_async_copy(stack.at[shard - start, :, pl.ds(part, w)], tiles.at[i], sem.at[i]).start()

        return carry

    lax.fori_loop(0, count, fetch, 0)
    sums[...] = jnp.zeros_like(sums) if first else sums_in[...]

    def rows(p):
        return slice(p * 2 * w, (p + 1) * 2 * w)

    def one(i):
        left, right = field(i, LEFT), field(i, RIGHT)
        hi, lo = split(tiles[i])
        half = jnp.concatenate([hi, lo], axis=1)
        wt = jnp.concatenate([half, half], axis=0)
        acc = None
        for p in range(pairs):
            h = jnp.dot(f2[left, rows(p), :], wt, preferred_element_type=f32)
            hi, lo = split(h[:, :w] + h[:, w:])
            lhs = jnp.concatenate(
                [jnp.concatenate([hi[:w], hi[w:]], axis=1), jnp.concatenate([lo[:w], lo[w:]], axis=1)], axis=0
            )
            d = jnp.dot(lhs, f2[right, rows(p), :], preferred_element_type=f32)
            acc = d if acc is None else acc + d
        part = acc[:w] + acc[w:]
        part = part[:, :w] + part[:, w:]
        for row, column, value in ((ROW_A, PART_A, part), (ROW_B, PART_B, part.T)):
            at, c = field(i, row), pl.ds(pl.multiple_of(field(i, column) * w, w), w)
            sums[at, :, c] = sums[at, :, c] + value

    def several(start, n):
        for k in range(n):
            pltpu.make_async_copy(stacks[0].at[0, :, pl.ds(0, w)], tiles.at[start + k], sem.at[start + k]).wait()
        for k in range(n):
            one(start + k)

    def many(i, carry):
        several(i * UNROLL, UNROLL)
        return carry

    def single(i, carry):
        several(i, 1)
        return carry

    lax.fori_loop(0, count // UNROLL, many, 0)
    done = count // UNROLL * UNROLL

    @pl.when(count - done >= 2)
    def _():
        several(done, 2)

    lax.fori_loop(count // 2 * 2, count, single, 0)
    for (start, size), out in zip(cuts, outs):
        out[...] = sums[start : start + size]


def run_stage(plan, tasks, stage, f2, stacks, firsts, sums, shape, cuts, keep):
    w = f2.shape[2] // 2
    first = sums is None
    vmem = pl.BlockSpec(memory_space=pltpu.VMEM)
    shapes = ([shape] if keep else []) + [(size,) + shape[1:] for _, size in cuts]
    outs = [jax.ShapeDtypeStruct(s, jnp.float32) for s in shapes]
    body = functools.partial(task_kernel, stage, first, keep, tuple(firsts), tuple(cuts))
    return pl.pallas_call(
        body,
        in_specs=[pl.BlockSpec(memory_space=pltpu.SMEM)] + [vmem] * (1 if first else 2)
        + [pl.BlockSpec(memory_space=pl.ANY)] * len(stacks),
        out_specs=[vmem] * len(outs),
        out_shape=outs,
        scratch_shapes=([] if keep else [pltpu.VMEM(shape, jnp.float32)]) + [
            pltpu.VMEM((tasks, w, w), jnp.float32),
            pltpu.SemaphoreType.DMA((tasks,)),
        ],
        compiler_params=pltpu.CompilerParams(vmem_limit_bytes=12 * MIB),
        cost_estimate=pl.CostEstimate(flops=tasks * f2.shape[1] * w * w * 4, bytes_accessed=2 * f2.size, transcendentals=0),
    )(plan, f2, *([] if first else [sums]), *stacks)


def shift(value, sizes, move):
    depth, wide, tall, cores = sizes
    pairs = []
    for source in range(depth * wide * tall * cores):
        rest, c = divmod(source, cores)
        rest, y = divmod(rest, tall)
        z, x = divmod(rest, wide)
        tz, tx, ty, tc = move(z, x, y, c)
        pairs.append((source, (((tz % depth) * wide + tx) * tall + ty) * cores + tc))
    return lax.ppermute(value, AXES, pairs)


def across_x(z, x, y, c):
    return z, 1 - x, y, c


def across_y(z, x, y, c):
    return z, x, 1 - y, c


def across_core(z, x, y, c):
    return z, x, y, 1 - c


def across_diagonal(z, x, y, c):
    return (z, x, 1 - y, c) if c == 0 else (z, 1 - x, y, c)


def across_z(step):
    return lambda z, x, y, c: (z ^ step, x, y, c)


def gathered(
    density,
    factors,
    orthogonalizers,
    slot_pairs,
    density_source,
    density_column,
    target_row,
    target_column,
):
    tiles_all = lax.axis_size("tile")
    aux_count = lax.axis_size("aux")
    tile_me = lax.axis_index("tile")
    aux_me = lax.axis_index("aux")
    tile_width = factors.shape[-1]
    task_count = slot_pairs.shape[0]
    per_block = tiles_all // aux_count
    depth = tiles_all // 2
    chunks = depth // 2
    sizes = (depth, 2, aux_count // 2, 2)
    on_first = (aux_me & 1) == 0

    def move(value, how):
        return shift(value, sizes, how)

    column = [density] + [move(density, across_z(step)) for step in range(1, depth)]
    tables = (density_source, density_column, target_row, target_column)
    plan, split_factors = prepare(depth, per_block, aux_count, tables, slot_pairs, factors)
    begin = waves_of(chunks)
    waves = [[], [], [], []]
    for k in range(chunks):
        here = jnp.stack(column[2 * k : 2 * k + 2])
        if k == 0:
            here, split_factors, on_first = lax.optimization_barrier((here, split_factors, on_first))
        side_x = move(here, across_x)
        side_y = move(here, across_y)
        corner = move(jnp.where(on_first, side_x, side_y), across_diagonal)
        first = int(k > 0)
        waves[first].append(here)
        waves[first + 1].extend((side_x, side_y))
        waves[first + 2].append(corner)
    by_stage = []
    for stage, parts in enumerate(waves):
        wave = jnp.concatenate(parts) if len(parts) > 1 else parts[0]
        by_stage.append(([wave, move(wave, across_core)], [begin[stage], begin[stage] + 4 * depth]))

    for known in range(2):
        by_stage[1][known].extend(by_stage[0][known])
        by_stage[2][known].extend(by_stage[1][known])
    by_stage.append(tuple(one + other for one, other in zip(by_stage[2], by_stage[3])))
    shape = (8 * depth,) + density.shape
    corner_cuts = [(at, depth) for at in (0, 4 * depth)]
    groups = [(depth + 4 * k, 4) for k in range(chunks)] + [(3 * depth + 2 * k, 2) for k in range(chunks)]
    cuts = groups + [(4 * depth + at, size) for at, size in groups]
    sums = None
    for stage, (values, firsts) in enumerate(by_stage):
        cut = {3: corner_cuts, 4: cuts}.get(stage, ())
        results = run_stage(plan, task_count, stage, split_factors, values, firsts, sums, shape, cut, stage < 4)
        sums = results[0]
        if stage == 3:
            corner_mine, corner_other = results[1:]
    mine, others = results[: len(groups)], results[len(groups) :]

    corner = corner_mine + move(corner_other, across_core)
    merged = [a + move(b, across_core) for a, b in zip(mine, others)]
    corners = [move(corner[2 * k : 2 * k + 2], across_diagonal) for k in range(chunks)]
    total = None
    for k in range(chunks):
        sides, here = merged[k], merged[chunks + k]
        side_x = sides[:2] + jnp.where(on_first, corners[k], 0.0)
        side_y = sides[2:] + jnp.where(on_first, 0.0, corners[k])
        here = here + move(side_x, across_x) + move(side_y, across_y)
        for bit in range(2):
            step = (chunks - 1 - k) * 2 + bit
            value = move(here[bit], across_z(step)) if step else here[bit]
            total = value if total is None else total + value

    blocks_x = orthogonalizers.reshape(tiles_all, tile_width, tile_width)
    left_x = blocks_x[tile_me]
    right_x = lax.dynamic_slice_in_dim(blocks_x, aux_me * per_block, per_block, 0)
    leftward = jnp.einsum("ki,kn->in", left_x, total, precision=highest)
    leftward = leftward.reshape(tile_width, per_block, tile_width)
    fock = jnp.einsum("ibl,blj->ibj", leftward, right_x, precision=highest)
    return fock.reshape(tile_width, per_block * tile_width)


def local(density, *rest):
    tiles_all = lax.axis_size("tile")
    aux_count = lax.axis_size("aux")
    whole = density.size * density.dtype.itemsize * tiles_all * aux_count
    cube = aux_count == 4 and LANES % rest[2].shape[0] == 0 and tiles_all >= aux_count and tiles_all & (tiles_all - 1) == 0
    if cube and whole <= GATHER_LIMIT:
        return gathered(density, *rest)
    return routed(density, *rest)


def solution(mesh):
    return jax.shard_map(
        local,
        mesh=mesh,
        in_specs=(
            P("tile", "aux"),
            P(("tile", "aux"), None, None, None),
            P(),
            P(("tile", "aux"), None),
            P(),
            P(),
            P(),
            P(),
        ),
        out_specs=P("tile", "aux"),
        check_vma=False,
    )
```

```python
import functools

import jax
import jax.numpy as jnp
from jax import lax
from jax.experimental import pallas as pl
from jax.experimental.pallas import tpu as pltpu
from jax.sharding import PartitionSpec as P


highest = lax.Precision.HIGHEST
AXES = ("tile", "aux")
GATHER_LIMIT = 16 << 20


def ranks_of(key_rows):
    task_count = key_rows.shape[-1]
    position = jnp.arange(task_count)
    earlier = position[None, :] < position[:, None]
    matching = key_rows[..., :, None] == key_rows[..., None, :]
    return jnp.sum(matching & earlier, axis=-1)


def slot_table(key_rows, other_rows, wanted, capacity):
    ranking = ranks_of(key_rows)
    levels = jnp.arange(capacity)
    chosen = (key_rows == wanted)[..., None, :] & (ranking[..., None, :] == levels[:, None])
    picked = jnp.sum(jnp.where(chosen, other_rows[..., None, :], 0), axis=-1)
    filled = jnp.any(chosen, axis=-1)
    return (picked, filled)


def routed(
    density,
    factors,
    orthogonalizers,
    slot_pairs,
    density_source,
    density_column,
    target_row,
    target_column,
):
    tiles_all = lax.axis_size("tile")
    aux_count = lax.axis_size("aux")
    tile_me = lax.axis_index("tile")
    aux_me = lax.axis_index("aux")
    tile_width = factors.shape[-1]
    task_count = slot_pairs.shape[0]
    capacity = max(2, 2 * task_count // tiles_all)
    quarter = tile_width // aux_count
    per_block = tiles_all // aux_count
    source_grid = density_source.reshape(tiles_all, aux_count, task_count)
    column_grid = density_column.reshape(tiles_all, aux_count, task_count)
    target_grid = target_row.reshape(tiles_all, aux_count, task_count)
    target_cols = target_column.reshape(tiles_all, aux_count, task_count)
    own_source = source_grid[tile_me, aux_me]
    own_target = target_grid[tile_me, aux_me]
    row_slab = lax.all_gather(density, "aux", axis=1, tiled=True)
    slab_tiles = row_slab.reshape(tile_width, tiles_all, tile_width)
    group_source = lax.dynamic_index_in_dim(source_grid, aux_me, 1, False)
    group_column = lax.dynamic_index_in_dim(column_grid, aux_me, 1, False)
    send_cols, send_filled = slot_table(group_source, group_column, tile_me, capacity)
    outgoing = jnp.take(slab_tiles, send_cols, axis=1)
    outgoing = jnp.where(send_filled[None, :, :, None], outgoing, 0.0)
    incoming = lax.all_to_all(outgoing, "tile", split_axis=1, concat_axis=1, tiled=True)
    own_rank = ranks_of(own_source)
    group = 8
    batches = task_count // group

    def one_batch(items):
        sources, rank_block, lefts, rights = items
        dens_block = incoming[:, sources, rank_block, :]
        halfway = jnp.einsum("gpik,kgl->gpil", factors[lefts], dens_block, precision=highest)
        return jnp.einsum("gpil,gplj->gij", halfway, factors[rights], precision=highest)

    partials = lax.map(
        one_batch,
        (
            own_source.reshape(batches, group),
            own_rank.reshape(batches, group),
            slot_pairs[:, 0].reshape(batches, group),
            slot_pairs[:, 1].reshape(batches, group),
        ),
    )
    partials = partials.reshape(task_count, tile_width, tile_width)
    task_ids = jnp.arange(task_count, dtype=jnp.int32)
    owners = jnp.arange(tiles_all, dtype=jnp.int32)[:, None]
    send_task, send_live = slot_table(own_target[None, :], task_ids[None, :], owners, capacity)
    outbound = jnp.where(send_live[:, :, None, None], partials[send_task], 0.0)
    arrived = lax.all_to_all(outbound, "tile", split_axis=0, concat_axis=0, tiled=True)
    group_target = lax.dynamic_index_in_dim(target_grid, aux_me, 1, False)
    group_cols = lax.dynamic_index_in_dim(target_cols, aux_me, 1, False)
    cols_b, cols_live = slot_table(group_target, group_cols, tile_me, capacity)
    spread = ((cols_b.reshape(-1)[None, :] == owners) & cols_live.reshape(-1)[None, :]).astype(
        jnp.float32
    )
    row_sums = jnp.einsum(
        "bs,sij->ibj", spread, arrived.reshape(-1, tile_width, tile_width), precision=highest
    )
    row_sums = row_sums.reshape(tile_width, tiles_all * tile_width)
    exchange_rows = lax.psum_scatter(row_sums, "aux", scatter_dimension=0, tiled=True)
    mirrored = lax.all_to_all(
        lax.all_to_all(
            exchange_rows.reshape(quarter, tiles_all, tile_width),
            "tile",
            split_axis=1,
            concat_axis=1,
            tiled=True,
        ),
        "aux",
        split_axis=1,
        concat_axis=0,
        tiled=True,
    )
    full_rows = lax.all_to_all(
        exchange_rows.reshape(quarter, aux_count, per_block * tile_width),
        "aux",
        split_axis=1,
        concat_axis=0,
        tiled=True,
    )
    direct_part = full_rows.reshape(tile_width, per_block, tile_width)
    symmetric = direct_part + jnp.transpose(mirrored, (2, 1, 0))
    blocks_x = orthogonalizers.reshape(tiles_all, tile_width, tile_width)
    left_x = blocks_x[tile_me]
    right_x = lax.dynamic_slice_in_dim(blocks_x, aux_me * per_block, per_block, 0)
    leftward = jnp.einsum("ki,kbl->ibl", left_x, symmetric, precision=highest)
    fock = jnp.einsum("ibl,blj->ibj", leftward, right_x, precision=highest)
    return fock.reshape(tile_width, per_block * tile_width)


MIB = 1 << 20
UNROLL = 4
LANES = 128
STAGES = 5
FIELDS = 8
LEFT, RIGHT, STACK, PART, ROW_A, PART_A, ROW_B, PART_B = range(FIELDS)


def split(x):
    hi = x.astype(jnp.bfloat16)
    lo = (x - hi.astype(jnp.float32)).astype(jnp.bfloat16)
    return hi, lo


def waves_of(chunks):
    return [0, 2, 4 + 2 * chunks, 2 + 6 * chunks]


def plan_tasks(depth, per_block, aux_count, source, column, row, target, pairs, plan):
    tasks = pairs.shape[1]
    width = plan.shape[1]
    chunks = depth // 2
    begin = waves_of(chunks)
    tile_me, aux_me = lax.axis_index("tile"), lax.axis_index("aux")
    z_me, x_me, y_me, c_me = tile_me >> 1, tile_me & 1, aux_me >> 1, aux_me & 1
    start = (tile_me * aux_count + aux_me) * tasks
    where, f32 = jnp.where, jnp.float32

    def own(table):
        line = table[pl.ds(lax.div(start, LANES), 1), :]
        return pltpu.roll(line, lax.rem(LANES - lax.rem(start, LANES), LANES), 1)[:, :tasks]

    def place(a, b):
        aux = lax.div(b, jnp.full_like(b, per_block))
        side = (((aux >> 1) ^ y_me) << 1) | ((a & 1) ^ x_me)
        return (aux & 1) ^ c_me, (a >> 1) ^ z_me, side, b - aux * per_block

    def target_of(a, b):
        dc, dz, side, part = place(a, b)
        turn = (chunks - 1 - (dz >> 1)) * 2
        straight = where(side == 0, 3 * depth, 0) + turn + (dz & 1)
        sideways = depth + turn * 2 + (side - 1) * 2 + (dz & 1)
        at = where((side == 1) | (side == 2), sideways, straight)
        return where(side == 3, 1, 0), dc * 4 * depth + at, part

    dc, dz, side, part = place(own(source), own(column))
    far = dz >> 1
    near_at = where(side == 0, begin[0], where(side == 3, begin[2], 2 * side))
    far_at = where(side == 0, begin[1] + 2 + 2 * far, where(side == 3, begin[3] - 2 + 2 * far, begin[2] - 4 + 4 * far + 2 * side))
    stack = dc * 4 * depth + where(far == 0, near_at, far_at) + (dz & 1)
    wave = where(side > 0, 1, 0) + where(side == 3, 1, 0) + where(far > 0, 1, 0)
    a, b = own(row), own(target)
    corner_a, row_a, part_a = target_of(a, b)
    corner_b, row_b, part_b = target_of(b, a)
    urgent = corner_a | corner_b

    above = lax.broadcasted_iota(jnp.int32, (tasks, tasks), 0)
    along = lax.broadcasted_iota(jnp.int32, (tasks, tasks), 1)

    def upright(line):
        return jnp.sum(where(above == along, line.astype(f32), 0.0), axis=1, keepdims=True)

    place_in = lax.broadcasted_iota(jnp.int32, (1, tasks), 1)
    key = (place_in + (1 - urgent) * tasks).astype(f32)
    before = where(upright(key) < key, 1.0, 0.0)

    def rank(which):
        return jnp.sum(before * upright(which), axis=0, keepdims=True)

    first = where(wave == 0, 1, 0)

    def most(which, top):
        n = jnp.sum(which.astype(f32), axis=1, keepdims=True)
        groups = jnp.floor(n / UNROLL) * UNROLL
        return where(n < UNROLL, n, jnp.minimum(groups, top))

    first = where(rank(first) < most(first, tasks // 4), first, 0)
    second = where(wave <= 1, 1 - first, 0)
    second = where(rank(second) < most(second, tasks * 3 // 8), second, 0)
    late = where(urgent > 0, jnp.maximum(wave, 2), 4)
    stage = where(first > 0, 0, where(second > 0, 1, late))
    stage_up = upright(stage)
    earlier = where(above < along, 1.0, 0.0)
    turn = jnp.sum(where(stage_up == stage.astype(f32), earlier, 0.0), axis=0, keepdims=True)
    slot_up = upright(stage.astype(f32) * tasks + turn)
    slots = lax.broadcasted_iota(jnp.int32, (tasks, width), 1)
    slots = slots.astype(f32)
    chosen = where(slot_up == slots, 1.0, 0.0).astype(jnp.bfloat16)
    values = jnp.zeros((FIELDS, tasks), jnp.int32)
    lines = lax.broadcasted_iota(jnp.int32, (FIELDS, tasks), 0)
    for f, value in enumerate((pairs[0:1, :], pairs[1:2, :], stack, part, row_a, part_a, row_b, part_b)):
        values = where(lines == f, value, values)
    listed = jnp.dot(values.astype(f32).astype(jnp.bfloat16), chosen, preferred_element_type=f32)
    plan[:FIELDS, :] = listed.astype(jnp.int32)
    lowest = stage_up * tasks
    inside = where(lowest <= slots, 1.0, 0.0) * where(slots < lowest + tasks, 1.0, 0.0)
    counts = jnp.sum(inside, axis=0, keepdims=True)
    plan[FIELDS:, :] = jnp.broadcast_to(counts, (FIELDS, width)).astype(jnp.int32)


def prepare_kernel(depth, per_block, aux_count, *refs):
    f_hbm, plan, o_ref, buf, sem = refs[5:]
    slots, rows, w = f_hbm.shape
    copies = [pltpu.make_async_copy(f_hbm.at[s], buf.at[s], sem.at[s]) for s in range(slots)]
    for copy in copies:
        copy.start()
    plan_tasks(depth, per_block, aux_count, *refs[:5], plan)
    step = 256
    for s, copy in enumerate(copies):
        copy.wait()

        @pl.loop(0, rows // step)
        def _(i, s=s):
            at = pl.ds(pl.multiple_of(i * step, step), step)
            hi, lo = split(buf[s, at, :])
            o_ref[s, at, :w] = hi
            o_ref[s, at, w:] = lo


def prepare(depth, per_block, aux_count, tables, pairs, factors):
    s, p, w, _ = factors.shape
    rows = p * w
    tasks = pairs.shape[0]
    vmem = pl.BlockSpec(memory_space=pltpu.VMEM)
    width = -(-STAGES * tasks // LANES) * LANES
    return pl.pallas_call(
        functools.partial(prepare_kernel, depth, per_block, aux_count),
        in_specs=[vmem] * 5 + [pl.BlockSpec(memory_space=pltpu.HBM)],
        out_specs=[vmem, vmem],
        out_shape=[
            jax.ShapeDtypeStruct((2 * FIELDS, width), jnp.int32),
            jax.ShapeDtypeStruct((s, rows, 2 * w), jnp.bfloat16),
        ],
        scratch_shapes=[
            pltpu.VMEM((s, rows, w), jnp.float32),
            pltpu.SemaphoreType.DMA((s,)),
        ],
        compiler_params=pltpu.CompilerParams(vmem_limit_bytes=8 * MIB),
        cost_estimate=pl.CostEstimate(flops=2 * factors.size, bytes_accessed=8 * factors.size, transcendentals=0),
    )(
        *(pltpu.with_memory_space_constraint(table.reshape(-1, LANES), pltpu.HBM) for table in tables),
        pltpu.with_memory_space_constraint(pairs.T, pltpu.HBM),
        pltpu.with_memory_space_constraint(factors.reshape(s, rows, w), pltpu.HBM),
    )


def task_kernel(stage, first, keep, firsts, cuts, plan, *refs):
    f2, *refs = refs
    if not first:
        sums_in, *refs = refs
    stacks, refs = refs[: len(firsts)], refs[len(firsts) :]
    if keep:
        sums, *refs = refs
    outs, refs = refs[: len(cuts)], refs[len(cuts) :]
    if not keep:
        sums, *refs = refs
    tiles, sem = refs
    w = f2.shape[2] // 2
    pairs = f2.shape[1] // (2 * w)
    f32 = jnp.float32

    tasks = tiles.shape[0]
    count = plan[FIELDS, stage * tasks]

    def field(i, f):
        return plan[f, stage * tasks + i]

    def fetch(i, carry):
        shard, part = field(i, STACK), pl.multiple_of(field(i, PART) * w, w)
        for start, stack in zip(firsts, stacks):
            @pl.when((shard >= start) & (shard < start + stack.shape[0]))
            def _(start=start, stack=stack):
                pltpu.make_async_copy(stack.at[shard - start, :, pl.ds(part, w)], tiles.at[i], sem.at[i]).start()

        return carry

    lax.fori_loop(0, count, fetch, 0)
    sums[...] = jnp.zeros_like(sums) if first else sums_in[...]

    def rows(p):
        return slice(p * 2 * w, (p + 1) * 2 * w)

    def weights(i):
        hi, lo = split(tiles[i])
        half = jnp.concatenate([hi, lo], axis=1)
        return jnp.concatenate([half, half], axis=0)

    def several(start, n):
        for i in range(n):
            pltpu.make_async_copy(stacks[0].at[0, :, pl.ds(0, w)], tiles.at[start + i], sem.at[start + i]).wait()
        kept = [weights(start + i) for i in range(n)]
        totals, waiting = [None] * n, []

        def second(i, p, h):
            hi, lo = split(h[:, :w] + h[:, w:])
            lhs = jnp.concatenate(
                [jnp.concatenate([hi[:w], hi[w:]], axis=1), jnp.concatenate([lo[:w], lo[w:]], axis=1)], axis=0
            )
            d = jnp.dot(lhs, f2[field(start + i, RIGHT), rows(p), :], preferred_element_type=f32)
            totals[i] = d if totals[i] is None else totals[i] + d

        for p in range(pairs):
            for i in range(n):
                h = jnp.dot(f2[field(start + i, LEFT), rows(p), :], kept[i], preferred_element_type=f32)
                waiting.append((i, p, h))
                if len(waiting) > n + 2:
                    second(*waiting.pop(0))
        for step in waiting:
            second(*step)
        for i, total in enumerate(totals):
            part = total[:w] + total[w:]
            part = part[:, :w] + part[:, w:]
            for row, column, value in ((ROW_A, PART_A, part), (ROW_B, PART_B, part.T)):
                at, c = field(start + i, row), pl.ds(pl.multiple_of(field(start + i, column) * w, w), w)
                sums[at, :, c] = sums[at, :, c] + value

    def many(i, carry):
        several(i * UNROLL, UNROLL)
        return carry

    def single(i, carry):
        several(i, 1)
        return carry

    lax.fori_loop(0, count // UNROLL, many, 0)
    done = count // UNROLL * UNROLL

    @pl.when(count - done >= 2)
    def _():
        several(done, 2)

    lax.fori_loop(count // 2 * 2, count, single, 0)
    for (start, size), out in zip(cuts, outs):
        out[...] = sums[start : start + size]


def run_stage(plan, tasks, stage, f2, stacks, firsts, sums, shape, cuts, keep):
    w = f2.shape[2] // 2
    first = sums is None
    vmem = pl.BlockSpec(memory_space=pltpu.VMEM)
    shapes = ([shape] if keep else []) + [(size,) + shape[1:] for _, size in cuts]
    outs = [jax.ShapeDtypeStruct(s, jnp.float32) for s in shapes]
    body = functools.partial(task_kernel, stage, first, keep, tuple(firsts), tuple(cuts))
    return pl.pallas_call(
        body,
        in_specs=[pl.BlockSpec(memory_space=pltpu.SMEM)] + [vmem] * (1 if first else 2)
        + [pl.BlockSpec(memory_space=pl.ANY)] * len(stacks),
        out_specs=[vmem] * len(outs),
        out_shape=outs,
        scratch_shapes=([] if keep else [pltpu.VMEM(shape, jnp.float32)]) + [
            pltpu.VMEM((tasks, w, w), jnp.float32),
            pltpu.SemaphoreType.DMA((tasks,)),
        ],
        compiler_params=pltpu.CompilerParams(vmem_limit_bytes=12 * MIB),
        cost_estimate=pl.CostEstimate(flops=tasks * f2.shape[1] * w * w * 4, bytes_accessed=2 * f2.size, transcendentals=0),
    )(plan, f2, *([] if first else [sums]), *stacks)


def shift(value, sizes, move):
    depth, wide, tall, cores = sizes
    pairs = []
    for source in range(depth * wide * tall * cores):
        rest, c = divmod(source, cores)
        rest, y = divmod(rest, tall)
        z, x = divmod(rest, wide)
        tz, tx, ty, tc = move(z, x, y, c)
        pairs.append((source, (((tz % depth) * wide + tx) * tall + ty) * cores + tc))
    return lax.ppermute(value, AXES, pairs)


def across_x(z, x, y, c):
    return z, 1 - x, y, c


def across_y(z, x, y, c):
    return z, x, 1 - y, c


def across_core(z, x, y, c):
    return z, x, y, 1 - c


def across_diagonal(z, x, y, c):
    return (z, x, 1 - y, c) if c == 0 else (z, 1 - x, y, c)


def across_z(step):
    return lambda z, x, y, c: (z ^ step, x, y, c)


def gathered(
    density,
    factors,
    orthogonalizers,
    slot_pairs,
    density_source,
    density_column,
    target_row,
    target_column,
):
    tiles_all = lax.axis_size("tile")
    aux_count = lax.axis_size("aux")
    tile_me = lax.axis_index("tile")
    aux_me = lax.axis_index("aux")
    tile_width = factors.shape[-1]
    task_count = slot_pairs.shape[0]
    per_block = tiles_all // aux_count
    depth = tiles_all // 2
    chunks = depth // 2
    sizes = (depth, 2, aux_count // 2, 2)
    on_first = (aux_me & 1) == 0

    def move(value, how):
        return shift(value, sizes, how)

    column = [density] + [move(density, across_z(step)) for step in range(1, depth)]
    tables = (density_source, density_column, target_row, target_column)
    plan, split_factors = prepare(depth, per_block, aux_count, tables, slot_pairs, factors)
    begin = waves_of(chunks)
    waves = [[], [], [], []]
    for k in range(chunks):
        here = jnp.stack(column[2 * k : 2 * k + 2])
        if k == 0:
            here, split_factors, on_first = lax.optimization_barrier((here, split_factors, on_first))
        side_x = move(here, across_x)
        side_y = move(here, across_y)
        corner = move(jnp.where(on_first, side_x, side_y), across_diagonal)
        first = int(k > 0)
        waves[first].append(here)
        waves[first + 1].extend((side_x, side_y))
        waves[first + 2].append(corner)
    by_stage = []
    for stage, parts in enumerate(waves):
        wave = jnp.concatenate(parts) if len(parts) > 1 else parts[0]
        by_stage.append(([wave, move(wave, across_core)], [begin[stage], begin[stage] + 4 * depth]))

    for known in range(2):
        by_stage[1][known].extend(by_stage[0][known])
        by_stage[2][known].extend(by_stage[1][known])
    by_stage.append(tuple(one + other for one, other in zip(by_stage[2], by_stage[3])))
    shape = (8 * depth,) + density.shape
    corner_cuts = [(at, depth) for at in (0, 4 * depth)]
    groups = [(depth + 4 * k, 4) for k in range(chunks)] + [(3 * depth + 2 * k, 2) for k in range(chunks)]
    cuts = groups + [(4 * depth + at, size) for at, size in groups]
    sums = None
    for stage, (values, firsts) in enumerate(by_stage):
        cut = {3: corner_cuts, 4: cuts}.get(stage, ())
        results = run_stage(plan, task_count, stage, split_factors, values, firsts, sums, shape, cut, stage < 4)
        sums = results[0]
        if stage == 3:
            corner_mine, corner_other = results[1:]
    mine, others = results[: len(groups)], results[len(groups) :]

    corner = corner_mine + move(corner_other, across_core)
    merged = [a + move(b, across_core) for a, b in zip(mine, others)]
    corner = move(corner, across_diagonal)
    corners = [corner[2 * k : 2 * k + 2] for k in range(chunks)]
    total = None
    for k in range(chunks):
        sides, here = merged[k], merged[chunks + k]
        side_x = sides[:2] + jnp.where(on_first, corners[k], 0.0)
        side_y = sides[2:] + jnp.where(on_first, 0.0, corners[k])
        here = here + move(side_x, across_x) + move(side_y, across_y)
        for bit in range(2):
            step = (chunks - 1 - k) * 2 + bit
            value = move(here[bit], across_z(step)) if step else here[bit]
            total = value if total is None else total + value

    blocks_x = orthogonalizers.reshape(tiles_all, tile_width, tile_width)
    left_x = blocks_x[tile_me]
    right_x = lax.dynamic_slice_in_dim(blocks_x, aux_me * per_block, per_block, 0)
    leftward = jnp.einsum("ki,kn->in", left_x, total, precision=highest)
    leftward = leftward.reshape(tile_width, per_block, tile_width)
    fock = jnp.einsum("ibl,blj->ibj", leftward, right_x, precision=highest)
    return fock.reshape(tile_width, per_block * tile_width)


def local(density, *rest):
    tiles_all = lax.axis_size("tile")
    aux_count = lax.axis_size("aux")
    whole = density.size * density.dtype.itemsize * tiles_all * aux_count
    cube = aux_count == 4 and LANES % rest[2].shape[0] == 0 and tiles_all >= aux_count and tiles_all & (tiles_all - 1) == 0
    if cube and whole <= GATHER_LIMIT:
        return gathered(density, *rest)
    return routed(density, *rest)


def solution(mesh):
    return jax.shard_map(
        local,
        mesh=mesh,
        in_specs=(
            P("tile", "aux"),
            P(("tile", "aux"), None, None, None),
            P(),
            P(("tile", "aux"), None),
            P(),
            P(),
            P(),
            P(),
        ),
        out_specs=P("tile", "aux"),
        check_vma=False,
    )
```

```python
import functools

import jax
import jax.numpy as jnp
from jax import lax
from jax.experimental import pallas as pl
from jax.experimental.pallas import tpu as pltpu
from jax.sharding import PartitionSpec as P


highest = lax.Precision.HIGHEST
AXES = ("tile", "aux")
GATHER_LIMIT = 16 << 20


def ranks_of(key_rows):
    task_count = key_rows.shape[-1]
    position = jnp.arange(task_count)
    earlier = position[None, :] < position[:, None]
    matching = key_rows[..., :, None] == key_rows[..., None, :]
    return jnp.sum(matching & earlier, axis=-1)


def slot_table(key_rows, other_rows, wanted, capacity):
    ranking = ranks_of(key_rows)
    levels = jnp.arange(capacity)
    chosen = (key_rows == wanted)[..., None, :] & (ranking[..., None, :] == levels[:, None])
    picked = jnp.sum(jnp.where(chosen, other_rows[..., None, :], 0), axis=-1)
    filled = jnp.any(chosen, axis=-1)
    return (picked, filled)


def routed(
    density,
    factors,
    orthogonalizers,
    slot_pairs,
    density_source,
    density_column,
    target_row,
    target_column,
):
    tiles_all = lax.axis_size("tile")
    aux_count = lax.axis_size("aux")
    tile_me = lax.axis_index("tile")
    aux_me = lax.axis_index("aux")
    tile_width = factors.shape[-1]
    task_count = slot_pairs.shape[0]
    capacity = max(2, 2 * task_count // tiles_all)
    quarter = tile_width // aux_count
    per_block = tiles_all // aux_count
    source_grid = density_source.reshape(tiles_all, aux_count, task_count)
    column_grid = density_column.reshape(tiles_all, aux_count, task_count)
    target_grid = target_row.reshape(tiles_all, aux_count, task_count)
    target_cols = target_column.reshape(tiles_all, aux_count, task_count)
    own_source = source_grid[tile_me, aux_me]
    own_target = target_grid[tile_me, aux_me]
    row_slab = lax.all_gather(density, "aux", axis=1, tiled=True)
    slab_tiles = row_slab.reshape(tile_width, tiles_all, tile_width)
    group_source = lax.dynamic_index_in_dim(source_grid, aux_me, 1, False)
    group_column = lax.dynamic_index_in_dim(column_grid, aux_me, 1, False)
    send_cols, send_filled = slot_table(group_source, group_column, tile_me, capacity)
    outgoing = jnp.take(slab_tiles, send_cols, axis=1)
    outgoing = jnp.where(send_filled[None, :, :, None], outgoing, 0.0)
    incoming = lax.all_to_all(outgoing, "tile", split_axis=1, concat_axis=1, tiled=True)
    own_rank = ranks_of(own_source)
    group = 8
    batches = task_count // group

    def one_batch(items):
        sources, rank_block, lefts, rights = items
        dens_block = incoming[:, sources, rank_block, :]
        halfway = jnp.einsum("gpik,kgl->gpil", factors[lefts], dens_block, precision=highest)
        return jnp.einsum("gpil,gplj->gij", halfway, factors[rights], precision=highest)

    partials = lax.map(
        one_batch,
        (
            own_source.reshape(batches, group),
            own_rank.reshape(batches, group),
            slot_pairs[:, 0].reshape(batches, group),
            slot_pairs[:, 1].reshape(batches, group),
        ),
    )
    partials = partials.reshape(task_count, tile_width, tile_width)
    task_ids = jnp.arange(task_count, dtype=jnp.int32)
    owners = jnp.arange(tiles_all, dtype=jnp.int32)[:, None]
    send_task, send_live = slot_table(own_target[None, :], task_ids[None, :], owners, capacity)
    outbound = jnp.where(send_live[:, :, None, None], partials[send_task], 0.0)
    arrived = lax.all_to_all(outbound, "tile", split_axis=0, concat_axis=0, tiled=True)
    group_target = lax.dynamic_index_in_dim(target_grid, aux_me, 1, False)
    group_cols = lax.dynamic_index_in_dim(target_cols, aux_me, 1, False)
    cols_b, cols_live = slot_table(group_target, group_cols, tile_me, capacity)
    spread = ((cols_b.reshape(-1)[None, :] == owners) & cols_live.reshape(-1)[None, :]).astype(
        jnp.float32
    )
    row_sums = jnp.einsum(
        "bs,sij->ibj", spread, arrived.reshape(-1, tile_width, tile_width), precision=highest
    )
    row_sums = row_sums.reshape(tile_width, tiles_all * tile_width)
    exchange_rows = lax.psum_scatter(row_sums, "aux", scatter_dimension=0, tiled=True)
    mirrored = lax.all_to_all(
        lax.all_to_all(
            exchange_rows.reshape(quarter, tiles_all, tile_width),
            "tile",
            split_axis=1,
            concat_axis=1,
            tiled=True,
        ),
        "aux",
        split_axis=1,
        concat_axis=0,
        tiled=True,
    )
    full_rows = lax.all_to_all(
        exchange_rows.reshape(quarter, aux_count, per_block * tile_width),
        "aux",
        split_axis=1,
        concat_axis=0,
        tiled=True,
    )
    direct_part = full_rows.reshape(tile_width, per_block, tile_width)
    symmetric = direct_part + jnp.transpose(mirrored, (2, 1, 0))
    blocks_x = orthogonalizers.reshape(tiles_all, tile_width, tile_width)
    left_x = blocks_x[tile_me]
    right_x = lax.dynamic_slice_in_dim(blocks_x, aux_me * per_block, per_block, 0)
    leftward = jnp.einsum("ki,kbl->ibl", left_x, symmetric, precision=highest)
    fock = jnp.einsum("ibl,blj->ibj", leftward, right_x, precision=highest)
    return fock.reshape(tile_width, per_block * tile_width)


MIB = 1 << 20
UNROLL = 4
LANES = 128
STAGES = 5
FIELDS = 8
LEFT, RIGHT, STACK, PART, ROW_A, PART_A, ROW_B, PART_B = range(FIELDS)


def split(x):
    hi = x.astype(jnp.bfloat16)
    lo = (x - hi.astype(jnp.float32)).astype(jnp.bfloat16)
    return hi, lo


def waves_of(chunks):
    return [0, 2, 4 + 2 * chunks, 2 + 6 * chunks]


def plan_tasks(depth, per_block, aux_count, source, column, row, target, pairs, plan):
    tasks = pairs.shape[1]
    width = plan.shape[1]
    chunks = depth // 2
    begin = waves_of(chunks)
    tile_me, aux_me = lax.axis_index("tile"), lax.axis_index("aux")
    z_me, x_me, y_me, c_me = tile_me >> 1, tile_me & 1, aux_me >> 1, aux_me & 1
    start = (tile_me * aux_count + aux_me) * tasks
    where, f32 = jnp.where, jnp.float32

    def own(table):
        line = table[pl.ds(lax.div(start, LANES), 1), :]
        return pltpu.roll(line, lax.rem(LANES - lax.rem(start, LANES), LANES), 1)[:, :tasks]

    def place(a, b):
        aux = lax.div(b, jnp.full_like(b, per_block))
        side = (((aux >> 1) ^ y_me) << 1) | ((a & 1) ^ x_me)
        return (aux & 1) ^ c_me, (a >> 1) ^ z_me, side, b - aux * per_block

    def target_of(a, b):
        dc, dz, side, part = place(a, b)
        turn = (chunks - 1 - (dz >> 1)) * 2
        straight = where(side == 0, 3 * depth, 0) + turn + (dz & 1)
        sideways = depth + turn * 2 + (side - 1) * 2 + (dz & 1)
        at = where((side == 1) | (side == 2), sideways, straight)
        return where(side == 3, 1, 0), dc * 4 * depth + at, part

    dc, dz, side, part = place(own(source), own(column))
    far = dz >> 1
    near_at = where(side == 0, begin[0], where(side == 3, begin[2], 2 * side))
    far_at = where(side == 0, begin[1] + 2 + 2 * far, where(side == 3, begin[3] - 2 + 2 * far, begin[2] - 4 + 4 * far + 2 * side))
    stack = dc * 4 * depth + where(far == 0, near_at, far_at) + (dz & 1)
    wave = where(side > 0, 1, 0) + where(side == 3, 1, 0) + where(far > 0, 1, 0)
    a, b = own(row), own(target)
    corner_a, row_a, part_a = target_of(a, b)
    corner_b, row_b, part_b = target_of(b, a)
    urgent = corner_a | corner_b

    above = lax.broadcasted_iota(jnp.int32, (tasks, tasks), 0)
    along = lax.broadcasted_iota(jnp.int32, (tasks, tasks), 1)

    def upright(line):
        return jnp.sum(where(above == along, line.astype(f32), 0.0), axis=1, keepdims=True)

    place_in = lax.broadcasted_iota(jnp.int32, (1, tasks), 1)
    key = (place_in + (1 - urgent) * tasks).astype(f32)
    before = where(upright(key) < key, 1.0, 0.0)

    def rank(which):
        return jnp.sum(before * upright(which), axis=0, keepdims=True)

    stage = where(urgent > 0, 3, 4)
    for known in range(3):
        open_now = where((wave <= known) & (stage > 2), 1.0, 0.0)
        found = jnp.sum(open_now, axis=1, keepdims=True)
        groups = jnp.floor(found / UNROLL) * UNROLL
        taken = jnp.minimum(where(found < UNROLL, found, groups) if known else found, tasks // 4)
        stage = where((open_now > 0) & (rank(open_now) < taken), known, stage)
    stage_up = upright(stage)
    earlier = where(above < along, 1.0, 0.0)
    turn = jnp.sum(where(stage_up == stage.astype(f32), earlier, 0.0), axis=0, keepdims=True)
    slot_up = upright(stage.astype(f32) * tasks + turn)
    slots = lax.broadcasted_iota(jnp.int32, (tasks, width), 1)
    slots = slots.astype(f32)
    chosen = where(slot_up == slots, 1.0, 0.0).astype(jnp.bfloat16)
    values = jnp.zeros((FIELDS, tasks), jnp.int32)
    lines = lax.broadcasted_iota(jnp.int32, (FIELDS, tasks), 0)
    for f, value in enumerate((pairs[0:1, :], pairs[1:2, :], stack, part, row_a, part_a, row_b, part_b)):
        values = where(lines == f, value, values)
    listed = jnp.dot(values.astype(f32).astype(jnp.bfloat16), chosen, preferred_element_type=f32)
    plan[:FIELDS, :] = listed.astype(jnp.int32)
    lowest = stage_up * tasks
    inside = where(lowest <= slots, 1.0, 0.0) * where(slots < lowest + tasks, 1.0, 0.0)
    counts = jnp.sum(inside, axis=0, keepdims=True)
    plan[FIELDS:, :] = jnp.broadcast_to(counts, (FIELDS, width)).astype(jnp.int32)


def prepare_kernel(depth, per_block, aux_count, *refs):
    f_hbm, plan, o_ref, buf, sem = refs[5:]
    slots, rows, w = f_hbm.shape
    copies = [pltpu.make_async_copy(f_hbm.at[s], buf.at[s], sem.at[s]) for s in range(slots)]
    for copy in copies:
        copy.start()
    plan_tasks(depth, per_block, aux_count, *refs[:5], plan)
    step = 256
    for s, copy in enumerate(copies):
        copy.wait()

        @pl.loop(0, rows // step)
        def _(i, s=s):
            at = pl.ds(pl.multiple_of(i * step, step), step)
            hi, lo = split(buf[s, at, :])
            o_ref[s, at, :w] = hi
            o_ref[s, at, w:] = lo


def prepare(depth, per_block, aux_count, tables, pairs, factors):
    s, p, w, _ = factors.shape
    rows = p * w
    tasks = pairs.shape[0]
    vmem = pl.BlockSpec(memory_space=pltpu.VMEM)
    width = -(-STAGES * tasks // LANES) * LANES
    return pl.pallas_call(
        functools.partial(prepare_kernel, depth, per_block, aux_count),
        in_specs=[vmem] * 5 + [pl.BlockSpec(memory_space=pltpu.HBM)],
        out_specs=[vmem, vmem],
        out_shape=[
            jax.ShapeDtypeStruct((2 * FIELDS, width), jnp.int32),
            jax.ShapeDtypeStruct((s, rows, 2 * w), jnp.bfloat16),
        ],
        scratch_shapes=[
            pltpu.VMEM((s, rows, w), jnp.float32),
            pltpu.SemaphoreType.DMA((s,)),
        ],
        compiler_params=pltpu.CompilerParams(vmem_limit_bytes=8 * MIB),
        cost_estimate=pl.CostEstimate(flops=2 * factors.size, bytes_accessed=8 * factors.size, transcendentals=0),
    )(
        *(pltpu.with_memory_space_constraint(table.reshape(-1, LANES), pltpu.HBM) for table in tables),
        pltpu.with_memory_space_constraint(pairs.T, pltpu.HBM),
        pltpu.with_memory_space_constraint(factors.reshape(s, rows, w), pltpu.HBM),
    )


def task_kernel(stage, first, keep, firsts, cuts, plan, *refs):
    f2, *refs = refs
    if not first:
        sums_in, *refs = refs
    stacks, refs = refs[: len(firsts)], refs[len(firsts) :]
    if keep:
        sums, *refs = refs
    outs, refs = refs[: len(cuts)], refs[len(cuts) :]
    if not keep:
        sums, *refs = refs
    tiles, sem = refs
    w = f2.shape[2] // 2
    pairs = f2.shape[1] // (2 * w)
    f32 = jnp.float32

    tasks = tiles.shape[0]
    count = plan[FIELDS, stage * tasks]

    def field(i, f):
        return plan[f, stage * tasks + i]

    def fetch(i, carry):
        shard, part = field(i, STACK), pl.multiple_of(field(i, PART) * w, w)
        for start, stack in zip(firsts, stacks):
            @pl.when((shard >= start) & (shard < start + stack.shape[0]))
            def _(start=start, stack=stack):
                pltpu.make_async_copy(stack.at[shard - start, :, pl.ds(part, w)], tiles.at[i], sem.at[i]).start()

        return carry

    lax.fori_loop(0, count, fetch, 0)
    sums[...] = jnp.zeros_like(sums) if first else sums_in[...]

    def rows(p):
        return slice(p * 2 * w, (p + 1) * 2 * w)

    def weights(i):
        hi, lo = split(tiles[i])
        half = jnp.concatenate([hi, lo], axis=1)
        return jnp.concatenate([half, half], axis=0)

    def several(start, n):
        for i in range(n):
            pltpu.make_async_copy(stacks[0].at[0, :, pl.ds(0, w)], tiles.at[start + i], sem.at[start + i]).wait()
        kept = [weights(start + i) for i in range(n)]
        totals, waiting = [None] * n, []

        def second(i, p, h):
            hi, lo = split(h[:, :w] + h[:, w:])
            lhs = jnp.concatenate(
                [jnp.concatenate([hi[:w], hi[w:]], axis=1), jnp.concatenate([lo[:w], lo[w:]], axis=1)], axis=0
            )
            d = jnp.dot(lhs, f2[field(start + i, RIGHT), rows(p), :], preferred_element_type=f32)
            totals[i] = d if totals[i] is None else totals[i] + d

        for p in range(pairs):
            for i in range(n):
                h = jnp.dot(f2[field(start + i, LEFT), rows(p), :], kept[i], preferred_element_type=f32)
                waiting.append((i, p, h))
                if len(waiting) > n + 2:
                    second(*waiting.pop(0))
        for step in waiting:
            second(*step)
        for i, total in enumerate(totals):
            part = total[:w] + total[w:]
            part = part[:, :w] + part[:, w:]
            for row, column, value in ((ROW_A, PART_A, part), (ROW_B, PART_B, part.T)):
                at, c = field(start + i, row), pl.ds(pl.multiple_of(field(start + i, column) * w, w), w)
                sums[at, :, c] = sums[at, :, c] + value

    def many(i, carry):
        several(i * UNROLL, UNROLL)
        return carry

    def single(i, carry):
        several(i, 1)
        return carry

    lax.fori_loop(0, count // UNROLL, many, 0)
    done = count // UNROLL * UNROLL

    @pl.when(count - done >= 2)
    def _():
        several(done, 2)

    lax.fori_loop(count // 2 * 2, count, single, 0)
    for (start, size), out in zip(cuts, outs):
        out[...] = sums[start : start + size]


def run_stage(plan, tasks, stage, f2, stacks, firsts, sums, shape, cuts, keep):
    w = f2.shape[2] // 2
    first = sums is None
    vmem = pl.BlockSpec(memory_space=pltpu.VMEM)
    shapes = ([shape] if keep else []) + [(size,) + shape[1:] for _, size in cuts]
    outs = [jax.ShapeDtypeStruct(s, jnp.float32) for s in shapes]
    body = functools.partial(task_kernel, stage, first, keep, tuple(firsts), tuple(cuts))
    return pl.pallas_call(
        body,
        in_specs=[pl.BlockSpec(memory_space=pltpu.SMEM)] + [vmem] * (1 if first else 2)
        + [pl.BlockSpec(memory_space=pl.ANY)] * len(stacks),
        out_specs=[vmem] * len(outs),
        out_shape=outs,
        scratch_shapes=([] if keep else [pltpu.VMEM(shape, jnp.float32)]) + [
            pltpu.VMEM((tasks, w, w), jnp.float32),
            pltpu.SemaphoreType.DMA((tasks,)),
        ],
        compiler_params=pltpu.CompilerParams(vmem_limit_bytes=12 * MIB),
        cost_estimate=pl.CostEstimate(flops=tasks * f2.shape[1] * w * w * 4, bytes_accessed=2 * f2.size, transcendentals=0),
    )(plan, f2, *([] if first else [sums]), *stacks)


def shift(value, sizes, move):
    depth, wide, tall, cores = sizes
    pairs = []
    for source in range(depth * wide * tall * cores):
        rest, c = divmod(source, cores)
        rest, y = divmod(rest, tall)
        z, x = divmod(rest, wide)
        tz, tx, ty, tc = move(z, x, y, c)
        pairs.append((source, (((tz % depth) * wide + tx) * tall + ty) * cores + tc))
    return lax.ppermute(value, AXES, pairs)


def across_x(z, x, y, c):
    return z, 1 - x, y, c


def across_y(z, x, y, c):
    return z, x, 1 - y, c


def across_core(z, x, y, c):
    return z, x, y, 1 - c


def across_diagonal(z, x, y, c):
    return (z, x, 1 - y, c) if c == 0 else (z, 1 - x, y, c)


def across_z(step):
    return lambda z, x, y, c: (z ^ step, x, y, c)


def gathered(
    density,
    factors,
    orthogonalizers,
    slot_pairs,
    density_source,
    density_column,
    target_row,
    target_column,
):
    tiles_all = lax.axis_size("tile")
    aux_count = lax.axis_size("aux")
    tile_me = lax.axis_index("tile")
    aux_me = lax.axis_index("aux")
    tile_width = factors.shape[-1]
    task_count = slot_pairs.shape[0]
    per_block = tiles_all // aux_count
    depth = tiles_all // 2
    chunks = depth // 2
    sizes = (depth, 2, aux_count // 2, 2)
    on_first = (aux_me & 1) == 0

    def move(value, how):
        return shift(value, sizes, how)

    column = [density] + [move(density, across_z(step)) for step in range(1, depth)]
    tables = (density_source, density_column, target_row, target_column)
    plan, split_factors = prepare(depth, per_block, aux_count, tables, slot_pairs, factors)
    begin = waves_of(chunks)
    waves = [[], [], [], []]
    for k in range(chunks):
        here = jnp.stack(column[2 * k : 2 * k + 2])
        if k == 0:
            here, split_factors, on_first = lax.optimization_barrier((here, split_factors, on_first))
        side_x = move(here, across_x)
        side_y = move(here, across_y)
        corner = move(jnp.where(on_first, side_x, side_y), across_diagonal)
        first = int(k > 0)
        waves[first].append(here)
        waves[first + 1].extend((side_x, side_y))
        waves[first + 2].append(corner)
    by_stage = []
    for stage, parts in enumerate(waves):
        wave = jnp.concatenate(parts) if len(parts) > 1 else parts[0]
        by_stage.append(([wave, move(wave, across_core)], [begin[stage], begin[stage] + 4 * depth]))

    for stage in range(3):
        by_stage[stage + 1] = [by_stage[stage][0] + by_stage[stage + 1][0], by_stage[stage][1] + by_stage[stage + 1][1]]
    by_stage.append(by_stage[3])
    shape = (8 * depth,) + density.shape
    corner_cuts = [(at, depth) for at in (0, 4 * depth)]
    groups = [(depth + 4 * k, 4) for k in range(chunks)] + [(3 * depth + 2 * k, 2) for k in range(chunks)]
    cuts = groups + [(4 * depth + at, size) for at, size in groups]
    sums = None
    for stage, (values, firsts) in enumerate(by_stage):
        cut = {3: corner_cuts, 4: cuts}.get(stage, ())
        results = run_stage(plan, task_count, stage, split_factors, values, firsts, sums, shape, cut, stage < 4)
        sums = results[0]
        if stage == 3:
            corner_mine, corner_other = results[1:]
    mine, others = results[: len(groups)], results[len(groups) :]

    corner = corner_mine + move(corner_other, across_core)
    merged = [a + move(b, across_core) for a, b in zip(mine, others)]
    corner = move(corner, across_diagonal)
    corners = [corner[2 * k : 2 * k + 2] for k in range(chunks)]
    total = None
    for k in range(chunks):
        sides, here = merged[k], merged[chunks + k]
        side_x = sides[:2] + jnp.where(on_first, corners[k], 0.0)
        side_y = sides[2:] + jnp.where(on_first, 0.0, corners[k])
        here = here + move(side_x, across_x) + move(side_y, across_y)
        for bit in range(2):
            step = (chunks - 1 - k) * 2 + bit
            value = move(here[bit], across_z(step)) if step else here[bit]
            total = value if total is None else total + value

    blocks_x = orthogonalizers.reshape(tiles_all, tile_width, tile_width)
    left_x = blocks_x[tile_me]
    right_x = lax.dynamic_slice_in_dim(blocks_x, aux_me * per_block, per_block, 0)
    leftward = jnp.einsum("ki,kn->in", left_x, total, precision=highest)
    leftward = leftward.reshape(tile_width, per_block, tile_width)
    fock = jnp.einsum("ibl,blj->ibj", leftward, right_x, precision=highest)
    return fock.reshape(tile_width, per_block * tile_width)


def local(density, *rest):
    tiles_all = lax.axis_size("tile")
    aux_count = lax.axis_size("aux")
    whole = density.size * density.dtype.itemsize * tiles_all * aux_count
    cube = aux_count == 4 and LANES % rest[2].shape[0] == 0 and tiles_all >= aux_count and tiles_all & (tiles_all - 1) == 0
    if cube and whole <= GATHER_LIMIT:
        return gathered(density, *rest)
    return routed(density, *rest)


def solution(mesh):
    return jax.shard_map(
        local,
        mesh=mesh,
        in_specs=(
            P("tile", "aux"),
            P(("tile", "aux"), None, None, None),
            P(),
            P(("tile", "aux"), None),
            P(),
            P(),
            P(),
            P(),
        ),
        out_specs=P("tile", "aux"),
        check_vma=False,
    )
```
